32 devices in a mesh: groups: 2 (over x), spots: 16 (over z, y, core).
Axes of the slice: x: 2, y: 2, z: 4, core: 2. Of those that a mesh axis runs over, the one named last changes fastest.
Arguments:
- influence: float32 [8, 512, 128, 128], P(None, ('groups', 'spots')), parts along dimension 1, may hold values from 0 to 0.008
- spot_weights: float32 [16384], P(('groups', 'spots')), parts along dimension 0, may hold values from 0.2 to 2
- vox_block: int32 [8, 512], P(None, ('groups', 'spots')), parts along dimension 1, may hold values from 0 to 63, as said below
- spot_block: int32 [8, 512], P(None, ('groups', 'spots')), parts along dimension 1, may hold values from 0 to 3
- labels: int32 [16384], P(('groups', 'spots')), parts along dimension 0, may hold values from 0 to 7
- importance: float32 [16384], P(('groups', 'spots')), parts along dimension 0, may hold values from 1 to 400
- prescription: float32 [16], P('groups'), parts along dimension 0, may hold values from 0.3 to 1.5
Outputs:
- soft_worst: float32 [16384], P(('groups', 'spots')), parts along dimension 0
- gradient: float32 [16384], P(('groups', 'spots')), parts along dimension 0
The draws below stay inside these ranges and needn't reach their ends.
There are 2 independent parts, one for each index of `groups`. The reference program is written for one: setup_inputs(seed, part) draws one part's arguments, and reference() takes and returns one part's arrays. A program takes and returns all parts, laid end to end along the dimension named above; each array names one. Nothing has to cross between parts.
Inputs may be any that keep to these rules, and one draw needn't show every extreme that they name: `vox_block`: device p of the spots axis holds the stored blocks p * 16 to (p + 1) * 16 - 1; the first of them in each scenario names a voxel block of the owner (p + 16 / 2) mod 16, every other one a voxel block of an owner at most 4 indices from p (no block below 0 or past the end).
All inputs are finite; a program needn't handle non-finite values.
Results may differ from the reference program's by a relative error of at most 0.0003.
Values sent between devices are 32-bit elements; how exact they have to be, the bound alone decides.
A program may use at most 64 MiB of HBM per device.

```python
import math
import jax
import jax.numpy as jnp
from jax import lax

S = 8
BV = 128
BS = 128
NLAB = 8
REACH = 4
SB_DEV = 4
NNZ_DEV = 16
VB_DEV = 4
SPOTS = 8192
VB_TOT = 64
VOXELS = 8192
NB_TOT = 256
N_SPOTS = 16


def draw_vox_block(key, part):
    owners = NB_TOT // NNZ_DEV
    slot_ids = jnp.arange(NB_TOT, dtype=jnp.int32)
    device_ids = jnp.broadcast_to((slot_ids // NNZ_DEV)[None, :], (S, NB_TOT))
    slot_within = jnp.broadcast_to((slot_ids % NNZ_DEV)[None, :], (S, NB_TOT))
    key_off = jax.random.fold_in(key, 11)
    key_row = jax.random.fold_in(key, 12)
    offsets = jax.random.randint(key_off, (S, NB_TOT), -REACH, REACH + 1, dtype=jnp.int32)
    near_ids = jnp.clip(device_ids + offsets, 0, owners - 1)
    mirror_ids = (device_ids + owners // 2) % owners
    owner_ids = jnp.where(slot_within == 0, mirror_ids, near_ids)
    row_ids = jax.random.randint(key_row, (S, NB_TOT), 0, VB_DEV, dtype=jnp.int32)
    return (owner_ids * VB_DEV + row_ids).astype(jnp.int32)


def draw_importance(key, part):
    unit = jax.random.uniform(key, (VOXELS,), jnp.float32)
    values = jnp.exp(unit * jnp.log(8.0))
    return jnp.clip(values, 1.0, 400.0).astype(jnp.float32)


def with_ends(array, stream_key, smallest, largest):
    place = [jax.random.randint(jax.random.fold_in(stream_key, axis), (), 0, length) for axis, length in enumerate(array.shape)]
    widest = array.shape.index(max(array.shape))
    next_to = place[:widest] + [(place[widest] + 1) % array.shape[widest]] + place[widest + 1:]
    return array.at[tuple(place)].set(smallest).at[tuple(next_to)].set(largest)


def level_of(own_key, dims, cuts, least, largest):
    gain, own = 1.0, jax.random.fold_in(own_key, 6)
    for position, blocks in cuts:
        heights = jnp.exp(jax.random.uniform(jax.random.fold_in(own, position), (blocks,), jnp.float32, least / len(cuts), largest / len(cuts)))
        gain = gain * jnp.repeat(heights, dims[position] // blocks).reshape([-1 if axis == position else 1 for axis in range(len(dims))])
    return gain


def setup_inputs(seed: int = 0, part: int = 0) -> dict:
    key_list = jax.random.split(jax.random.key(seed), 8)
    own_keys = jax.random.split(jax.random.fold_in(key_list[7], part), 8)
    return {
        "influence": jnp.clip(0.008 * jax.random.uniform(own_keys[0], (S, NB_TOT, BV, BS), jnp.float32) ** level_of(own_keys[0], (S, NB_TOT, BV, BS), ((1, 16),), -0.2, 0.2), 0.0, 0.008),
        "spot_weights": jnp.clip(jnp.exp(math.log(2.0) - 2.3025851 * jax.random.uniform(own_keys[1], (SPOTS,), jnp.float32) ** level_of(own_keys[1], (SPOTS,), ((0, 16),), -0.2, 0.2)), 0.2, 2.0),
        "vox_block": draw_vox_block(jax.random.fold_in(jax.random.fold_in(key_list[7], part), 71), part),
        "spot_block": with_ends(jax.random.randint(own_keys[3], (S, NB_TOT), 0, SB_DEV), jax.random.fold_in(own_keys[3], 1), 0, SB_DEV - 1).astype(jnp.int32),
        "labels": with_ends(jax.random.randint(own_keys[4], (VOXELS,), 0, NLAB), jax.random.fold_in(own_keys[4], 1), 0, NLAB - 1).astype(jnp.int32),
        "importance": draw_importance(jax.random.fold_in(jax.random.fold_in(key_list[7], part), 71), part),
        "prescription": jnp.clip(jax.random.uniform(own_keys[6], (NLAB,), jnp.float32, 0.3, 1.5), 0.3, 1.5),
    }


def reference(influence, spot_weights, vox_block, spot_block, labels, importance, prescription):
    high = lax.Precision.HIGHEST
    slot_ids = jnp.arange(NB_TOT, dtype=jnp.int32)
    spot_global = (slot_ids // NNZ_DEV)[None, :] * SB_DEV + spot_block
    weight_rows = spot_weights.reshape(SB_DEV * N_SPOTS, BS)
    slot_input = weight_rows[spot_global]
    slot_dose = jnp.einsum("snvk,snk->snv", influence, slot_input, precision=high)
    scen_ids = jnp.broadcast_to(jnp.arange(S, dtype=jnp.int32)[:, None], (S, NB_TOT))
    dose_field = jnp.zeros((VB_TOT, S, BV), jnp.float32).at[vox_block, scen_ids].add(slot_dose)
    target = prescription[labels].reshape(VB_TOT, 1, BV)
    imp_rows = importance.reshape(VB_TOT, 1, BV)
    excess = dose_field - target
    score = imp_rows * excess * excess
    soft_worst = jax.nn.logsumexp(score, axis=1).reshape(VOXELS)
    dose_coef = jax.nn.softmax(score, axis=1) * 2.0 * imp_rows * excess
    slot_coef = dose_coef[vox_block, scen_ids]
    slot_grad = jnp.einsum("snvk,snv->snk", influence, slot_coef, precision=high)
    gradient = jnp.zeros((SB_DEV * N_SPOTS, BS), jnp.float32).at[spot_global].add(slot_grad)
    return soft_worst, gradient.reshape(SPOTS)
```

```python
import functools

import jax
import jax.numpy as jnp
from jax import lax
from jax.experimental import pallas as pl
from jax.experimental.pallas import tpu as pltpu
from jax.sharding import PartitionSpec as P

REACH = 4
NEAR = 2 * REACH + 1
AHEAD = 4
F32 = jnp.float32
BF16 = jnp.bfloat16
MESH = pl.DeviceIdType.MESH


def split(x):
    hi = x.astype(BF16)
    lo = (x - hi.astype(F32)).astype(BF16)
    return hi, lo


def iota(shape, dim):
    return lax.broadcasted_iota(jnp.int32, shape, dim)


def kernel(
    inf_ref, w_in, vox_in, spot_in, lab_in, imp_in, presc_in,
    out_ref,
    w_ref, vox_ref, spot_ref, lab_ref, imp_ref, presc_ref, small_sem,
    land, ihi, ilo, part, recv, coef, cbuf, pick, keys,
    load_sem, sent, came,
):
    scen, slots, rows, cols = land.shape
    vr = lab_ref.shape[0]
    sb = w_ref.shape[0]
    two = 8 // vr
    pairs = scen // two
    dests = NEAR + 1
    qrows = dests * 8
    n = lax.axis_size("spots")
    me = lax.axis_index("spots")
    mirror = lax.rem(me + n // 2, n)

    def load_of(s):
        return pltpu.make_async_copy(inf_ref.at[s], land.at[s], load_sem.at[s % AHEAD])

    small = [
        pltpu.make_async_copy(src, dst, small_sem.at[i])
        for i, (src, dst) in enumerate((
            (w_in, w_ref), (vox_in, vox_ref), (spot_in, spot_ref),
            (lab_in, lab_ref), (imp_in, imp_ref), (presc_in, presc_ref),
        ))
    ]
    for load in small[:3] + [load_of(s) for s in range(AHEAD)] + small[3:]:
        load.start()

    near = [e for e in range(-REACH, REACH + 1) if e != 0]
    order = sorted(near, key=abs)

    def inside(e):
        return me + e >= 0 if e < 0 else me + e < n

    barrier = pltpu.get_barrier_semaphore()
    for e in near:
        @pl.when(inside(e))
        def _():
            pl.semaphore_signal(barrier, inc=1, device_id={"spots": me + e}, device_id_type=MESH)
    pl.semaphore_signal(barrier, inc=1, device_id={"spots": mirror}, device_id_type=MESH)

    for e in near:
        @pl.when(jnp.logical_not(inside(e)))
        def _():
            recv[e + REACH] = jnp.zeros(recv.shape[1:], F32)
            cbuf[e + REACH] = jnp.zeros(cbuf.shape[1:], F32)

    for load in small[:3]:
        load.wait()

    w_hi, w_lo = split(w_ref[...])
    w_rows = jnp.concatenate([w_hi.astype(F32), w_lo.astype(F32)], axis=0)
    parts = w_rows.shape[0]
    wide = 2 * cols
    none = jnp.zeros((parts, wide), F32)
    w_two = jnp.concatenate(
        [jnp.concatenate([w_rows, w_rows], axis=1), none], axis=0
    ).astype(BF16)
    width = slots * parts

    def one_hot(mask):
        return mask.astype(F32).astype(BF16)

    def push(rhs, unit, stage=0, transpose=False):
        pltpu.matmul_push_rhs(rhs, stage, unit, transpose=transpose)

    def rows_of(x, count):
        return jnp.concatenate([x, jnp.zeros((count - x.shape[0], x.shape[1]), x.dtype)], axis=0)

    def lanes_of(x, count):
        return jnp.concatenate([x, jnp.zeros((x.shape[0], count - x.shape[1]), x.dtype)], axis=1)

    vox = vox_ref[...]
    slot_id = iota(vox.shape, 1)
    rel = jnp.where(
        slot_id == 0,
        vox - vr * mirror + vr * NEAR,
        vox - vr * me + vr * REACH,
    )
    code = rows_of(lanes_of((rel * sb + spot_ref[...]).astype(F32), wide), wide).astype(BF16)

    def codes(acc, acc_t):
        push(one_hot(iota((wide, wide), 1) // parts == iota((wide, wide), 0)), 0)
        pltpu.matmul_acc_lhs(acc, code[:2 * scen], load_staged_rhs=0)
        push(code, 1, transpose=True)
        pltpu.matmul_acc_lhs(
            acc_t, one_hot(iota((width, wide), 0) // parts == iota((width, wide), 1)),
            load_staged_rhs=0,
        )
        return pltpu.matmul_pop(acc)[:scen, :width], pltpu.matmul_pop(acc_t)[:, :cols]

    key, key_t = pl.run_scoped(
        codes, pltpu.ACC(0)((2 * scen, wide), F32), pltpu.ACC(1)((width, wide), F32)
    )
    key = key.astype(jnp.int32) - iota((scen, width), 1) % sb
    key_t = key_t.astype(jnp.int32) - iota((width, cols), 0) % sb

    far = sb * vr * dests * 2

    def rel_of(q):
        return sb * ((q // 8) * vr + q % vr) + far * ((q % 8) // vr)

    row_code = rel_of(iota((qrows, two * width), 0))
    for sp in range(pairs):
        keys[sp] = jnp.concatenate(
            [key[sp * two + s2:sp * two + s2 + 1] + far * s2 for s2 in range(two)], axis=1
        )

    count = sum(inside(e).astype(jnp.int32) for e in near)
    counts = sorted({sum(0 <= m + e < n for e in near) for m in range(n)})

    def near_copy(src, dst, turn, e):
        return pltpu.make_async_remote_copy(
            src_ref=src(REACH + e), dst_ref=dst(REACH - e),
            send_sem=sent.at[turn], recv_sem=came.at[turn],
            device_id={"spots": me + e}, device_id_type=MESH,
        )

    def far_copy(src, dst, turn):
        return pltpu.make_async_remote_copy(
            src_ref=src(NEAR), dst_ref=dst(NEAR),
            send_sem=sent.at[turn], recv_sem=came.at[turn],
            device_id={"spots": mirror}, device_id_type=MESH,
        )

    def exchange(src, dst, turn):
        far_copy(src, dst, turn).start()
        for e in order:
            @pl.when(inside(e))
            def _():
                near_copy(src, dst, turn, e).start()

    def all_slabs(sem):
        for c in counts:
            @pl.when(count == c)
            def _():
                slabs = recv.at[pl.ds(0, c + 1)]
                pltpu.make_async_copy(slabs, slabs, sem).wait()

    def cut_of(ref, lo, size):
        return lambda i: ref.at[i, pl.ds(lo, size)]

    early = pairs - 1
    step = wide // rows

    def doses(sp, ahead):
        tiles = two * slots // step

        def tile_sums(*accs):
            for t in range(tiles):
                s2, b = divmod(t * step, slots)
                s = sp * two + s2
                if b == 0:
                    load_of(s).wait()
                    if ahead:
                        @pl.when(s + AHEAD < scen)
                        def _():
                            load_of(s + AHEAD).start()
                his, los = zip(*[split(land[s, b + k]) for k in range(step)])
                rhs = jnp.concatenate(
                    [jnp.concatenate(his, axis=0), jnp.concatenate(los, axis=0)], axis=1
                )
                push(rhs, t % 2, t // 2 % 2, transpose=True)
                pltpu.matmul_acc_lhs(accs[t], w_two, load_staged_rhs=t // 2 % 2)
            outs = []
            for t in range(tiles):
                got = pltpu.matmul_pop(accs[t])[:parts]
                outs += [got[:, k * rows:(k + 1) * rows] for k in range(step)]
            return jnp.concatenate(outs, axis=0)

        dose = pl.run_scoped(
            tile_sums, *[pltpu.ACC(t % 2)((2 * parts, wide), F32) for t in range(tiles)]
        )
        onto = one_hot(row_code == keys[sp])
        d1 = dose.astype(BF16)
        rest = dose - d1.astype(F32)
        d2, d3 = split(rest)

        def cell_sums(acc, low):
            push(jnp.concatenate([d1, d2], axis=1), 0)
            push(lanes_of(d3, wide), 1)
            pltpu.matmul_acc_lhs(acc, onto, load_staged_rhs=0)
            pltpu.matmul_acc_lhs(low, onto, load_staged_rhs=0)
            both, third = pltpu.matmul_pop(acc), pltpu.matmul_pop(low)
            return both[:, :rows] + (both[:, rows:] + third[:, :rows])

        total = pl.run_scoped(cell_sums, *[pltpu.ACC(u)((qrows, wide), F32) for u in range(2)])
        part[:, sp] = total.reshape(dests, 8, rows)

    def early_doses(sp, carry):
        doses(sp, True)
        return carry

    lax.fori_loop(0, early, early_doses, 0)
    pl.semaphore_wait(barrier, count + 1)
    exchange(cut_of(part, 0, early), cut_of(recv, 0, early), 0)
    doses(early, False)
    exchange(cut_of(part, early, 1), cut_of(recv, early, 1), 0)

    def keep(s, carry):
        for b in range(slots):
            hi, lo = split(land[s, b])
            ihi[s, pl.ds(b * rows, rows)] = hi
            ilo[s, pl.ds(b * rows, rows)] = lo
        return carry

    lax.fori_loop(0, scen, keep, 0)

    lane = iota((width, 2 * 128), 1)
    line = iota((width, 2 * 128), 0)
    q = lane % 128
    lane_code = jnp.where(
        jnp.logical_and(lane // 128 == (line % parts) // sb, q < qrows), rel_of(q), -1000
    )
    for s in range(scen):
        pick[s] = one_hot(key_t[:, s:s + 1] + far * (s % two) == lane_code)
    for load in small[3:]:
        load.wait()
    labels = lab_ref[...]
    target = jnp.zeros(labels.shape, F32)
    for k in range(presc_ref.shape[0]):
        target = jnp.where(labels == k, presc_ref[k], target)
    target = jnp.concatenate([target] * two, axis=0)
    imp = jnp.concatenate([imp_ref[...]] * two, axis=0)

    all_slabs(came.at[0])
    field = part[REACH]
    for i in range(dests):
        if i != REACH:
            field = field + recv[i]
    excess = field - target[None]
    score = imp[None] * excess * excess
    top = jnp.max(score, axis=0)
    top = jnp.maximum(top, pltpu.roll(top, vr, 0))
    expo = jnp.exp(score - top[None])
    whole = jnp.sum(expo, axis=0)
    whole = whole + pltpu.roll(whole, vr, 0)
    coef_now = expo / whole[None] * 2.0 * imp[None] * excess
    coef[...] = coef_now
    exchange(lambda i: coef, lambda i: cbuf.at[i], 1)
    out_ref[pl.ds(0, vr)] = (top + jnp.log(whole))[:vr]
    cbuf[REACH] = coef_now
    all_slabs(sent.at[0])

    all_slabs(came.at[1])
    pad = jnp.zeros((128 - qrows, rows), BF16)

    def picked(*accs):
        for sp in range(pairs):
            c_hi, c_lo = split(cbuf[:, sp].reshape(qrows, rows))
            c_two = jnp.concatenate([c_hi, pad, c_lo, pad], axis=0)
            push(lanes_of(c_two, wide), sp % 2, sp // 2)
            for s2 in range(two):
                pltpu.matmul_acc_lhs(
                    accs[sp * two + s2], pick[sp * two + s2],
                    **({"load_staged_rhs": sp // 2} if s2 == 0 else {}),
                )
        return [pltpu.matmul_pop(acc)[:, :rows] for acc in accs]

    lefts = pl.run_scoped(
        picked, *[pltpu.ACC(s // two % 2)((width, wide), F32) for s in range(scen)]
    )

    def gather(*sums):
        for t in range(scen * slots // step):
            s, b = divmod(t * step, slots)
            unit, stage = t % 2, t // 2 % 2
            block = pl.ds(b * rows, step * rows)
            push(jnp.concatenate([ihi[s, block], ilo[s, block]], axis=1), unit, stage)
            left = jnp.concatenate(
                [lefts[s][(b + k) * parts:(b + k + 1) * parts] for k in range(step)], axis=1
            )
            pltpu.matmul_acc_lhs(
                sums[unit], jnp.concatenate([left, none], axis=0).astype(BF16),
                load_staged_rhs=stage,
            )
        return (pltpu.matmul_pop(sums[0]) + pltpu.matmul_pop(sums[1]))[:parts]

    acc = pl.run_scoped(gather, *[pltpu.ACC(u)((2 * parts, wide), F32) for u in range(2)])
    acc = acc[:, :cols] + acc[:, cols:]
    out_ref[pl.ds(vr, sb)] = acc[:sb] + acc[sb:]

    all_slabs(sent.at[1])


def per_device(influence, spot_weights, vox_block, spot_block, labels, importance, prescription):
    scen, slots, rows, cols = influence.shape
    sb = spot_weights.shape[0] // cols
    vr = labels.shape[0] // rows
    assert 8 % vr == 0 and 2 * vr == 8 and scen % 2 == 0 and 2 * sb == 8
    slab = (scen * vr // 8, 8, rows)
    dests = NEAR + 1
    vmem = pl.BlockSpec(memory_space=pltpu.VMEM)
    both = pl.pallas_call(
        kernel,
        out_shape=pltpu.VMEM((vr + sb, rows), F32),
        in_specs=[pl.BlockSpec(memory_space=pl.ANY)] * 7,
        out_specs=vmem,
        scratch_shapes=[
            pltpu.VMEM((sb, cols), F32),
            pltpu.VMEM(vox_block.shape, jnp.int32),
            pltpu.VMEM(spot_block.shape, jnp.int32),
            pltpu.VMEM((vr, rows), jnp.int32),
            pltpu.VMEM((vr, rows), F32),
            pltpu.SMEM(prescription.shape, F32),
            pltpu.SemaphoreType.DMA((6,)),
            pltpu.VMEM((scen, slots, rows, cols), F32),
            pltpu.VMEM((scen, slots * rows, cols), BF16),
            pltpu.VMEM((scen, slots * rows, cols), BF16),
            pltpu.VMEM((dests,) + slab, F32),
            pltpu.VMEM((dests,) + slab, F32),
            pltpu.VMEM(slab, F32),
            pltpu.VMEM((dests,) + slab, F32),
            pltpu.VMEM((scen, slots * 2 * sb, 256), BF16),
            pltpu.VMEM((scen // 2, 1, 2 * slots * 2 * sb), jnp.int32),
            pltpu.SemaphoreType.DMA((AHEAD,)),
            pltpu.SemaphoreType.DMA((2,)),
            pltpu.SemaphoreType.DMA((2,)),
        ],
        compiler_params=pltpu.CompilerParams(
            collective_id=0, has_side_effects=True, vmem_limit_bytes=56 * 1024 * 1024
        ),
    )(
        influence, spot_weights.reshape(sb, cols), vox_block, spot_block,
        labels.reshape(vr, rows), importance.reshape(vr, rows), prescription,
    )
    return both[:vr].reshape(vr * rows), both[vr:].reshape(sb * cols)


def solution(mesh):
    both = P(("groups", "spots"))
    in_specs = (
        P(None, ("groups", "spots"), None, None),
        both,
        P(None, ("groups", "spots")),
        P(None, ("groups", "spots")),
        both,
        both,
        P("groups"),
    )
    return jax.shard_map(
        per_device, mesh=mesh, in_specs=in_specs, out_specs=(both, both), check_vma=False
    )
```

```python
import jax
import jax.numpy as jnp
from jax import lax
from jax.experimental import pallas as pl
from jax.experimental.pallas import tpu as pltpu
from jax.sharding import PartitionSpec as P

REACH = 4
NEAR = 2 * REACH + 1
AHEAD = 5
F32 = jnp.float32
BF16 = jnp.bfloat16
MESH = pl.DeviceIdType.MESH


def split(x):
    hi = x.astype(BF16)
    lo = (x - hi.astype(F32)).astype(BF16)
    return hi, lo


def iota(shape, dim):
    return lax.broadcasted_iota(jnp.int32, shape, dim)


def kernel(
    inf_ref, w_in, vox_in, spot_in, lab_in, imp_in, presc_in,
    out_ref,
    w_ref, vox_ref, spot_ref, lab_ref, imp_ref, presc_ref, small_sem,
    land, ihi, ilo, part, recv, coef, cbuf, pick, keys,
    load_sem, sent, came,
):
    scen, slots, rows, cols = land.shape
    vr = lab_ref.shape[0]
    sb = w_ref.shape[0]
    two = 8 // vr
    pairs = scen // two
    dests = NEAR + 1
    qrows = dests * 8
    n = lax.axis_size("spots")
    me = lax.axis_index("spots")
    mirror = lax.rem(me + n // 2, n)

    pieces = [(0, 0, slots // 4), (0, slots // 4, slots - slots // 4)]
    pieces += [(s, 0, slots) for s in range(1, scen - 1)]
    pieces += [(scen - 1, 0, slots // 2), (scen - 1, slots // 2, slots // 2)]

    def load_of(i):
        s, lo, size = pieces[i]
        block = (s, pl.ds(lo, size))
        return pltpu.make_async_copy(inf_ref.at[block], land.at[block], load_sem.at[i % AHEAD])

    small = [
        pltpu.make_async_copy(src, dst, small_sem.at[i])
        for i, (src, dst) in enumerate((
            (w_in, w_ref), (vox_in, vox_ref), (spot_in, spot_ref),
            (lab_in, lab_ref), (imp_in, imp_ref), (presc_in, presc_ref),
        ))
    ]
    for load in small[:3] + [load_of(s) for s in range(AHEAD)] + small[3:]:
        load.start()

    near = [e for e in range(-REACH, REACH + 1) if e != 0]
    order = sorted(near, key=lambda e: (-abs(e), e))

    def inside(e):
        return me + e >= 0 if e < 0 else me + e < n

    barrier = pltpu.get_barrier_semaphore()
    for e in near:
        @pl.when(inside(e))
        def _():
            pl.semaphore_signal(barrier, inc=1, device_id={"spots": me + e}, device_id_type=MESH)
    pl.semaphore_signal(barrier, inc=1, device_id={"spots": mirror}, device_id_type=MESH)

    for e in near:
        @pl.when(jnp.logical_not(inside(e)))
        def _():
            recv[e + REACH] = jnp.zeros(recv.shape[1:], F32)
            cbuf[e + REACH] = jnp.zeros(cbuf.shape[1:], F32)

    for load in small[:3]:
        load.wait()

    w_hi, w_lo = split(w_ref[...])
    w_rows = jnp.concatenate([w_hi.astype(F32), w_lo.astype(F32)], axis=0)
    parts = w_rows.shape[0]
    wide = 2 * cols
    none = jnp.zeros((parts, wide), F32)
    w_two = jnp.concatenate(
        [jnp.concatenate([w_rows, w_rows], axis=1), none], axis=0
    ).astype(BF16)
    width = slots * parts

    def one_hot(mask):
        return mask.astype(F32).astype(BF16)

    def push(rhs, unit, stage=0, transpose=False):
        pltpu.matmul_push_rhs(rhs, stage, unit, transpose=transpose)

    def rows_of(x, count):
        return jnp.concatenate([x, jnp.zeros((count - x.shape[0], x.shape[1]), x.dtype)], axis=0)

    def lanes_of(x, count):
        return jnp.concatenate([x, jnp.zeros((x.shape[0], count - x.shape[1]), x.dtype)], axis=1)

    vox = vox_ref[...]
    slot_id = iota(vox.shape, 1)
    rel = jnp.where(
        slot_id == 0,
        vox - vr * mirror + vr * NEAR,
        vox - vr * me + vr * REACH,
    )
    code = rows_of(lanes_of((rel * sb + spot_ref[...]).astype(F32), wide), wide).astype(BF16)

    def codes(acc, acc_t):
        push(one_hot(iota((wide, wide), 1) // parts == iota((wide, wide), 0)), 0)
        pltpu.matmul_acc_lhs(acc, code[:2 * scen], load_staged_rhs=0)
        push(code, 1, transpose=True)
        pltpu.matmul_acc_lhs(
            acc_t, one_hot(iota((width, wide), 0) // parts == iota((width, wide), 1)),
            load_staged_rhs=0,
        )
        return pltpu.matmul_pop(acc)[:scen, :width], pltpu.matmul_pop(acc_t)[:, :cols]

    key, key_t = pl.run_scoped(
        codes, pltpu.ACC(0)((2 * scen, wide), F32), pltpu.ACC(1)((width, wide), F32)
    )
    key = key.astype(jnp.int32) - iota((scen, width), 1) % sb
    key_t = key_t.astype(jnp.int32) - iota((width, cols), 0) % sb

    far = sb * vr * dests * 2

    def rel_of(q):
        return sb * ((q // 8) * vr + q % vr) + far * ((q % 8) // vr)

    row_code = rel_of(iota((qrows, two * width), 0))
    for sp in range(pairs):
        keys[sp] = jnp.concatenate(
            [key[sp * two + s2:sp * two + s2 + 1] + far * s2 for s2 in range(two)], axis=1
        )

    count = sum(inside(e).astype(jnp.int32) for e in near)
    counts = sorted({sum(0 <= m + e < n for e in near) for m in range(n)})

    def near_copy(src, dst, turn, e):
        return pltpu.make_async_remote_copy(
            src_ref=src(REACH + e), dst_ref=dst(REACH - e),
            send_sem=sent.at[turn], recv_sem=came.at[turn],
            device_id={"spots": me + e}, device_id_type=MESH,
        )

    def far_copy(src, dst, turn):
        return pltpu.make_async_remote_copy(
            src_ref=src(NEAR), dst_ref=dst(NEAR),
            send_sem=sent.at[turn], recv_sem=came.at[turn],
            device_id={"spots": mirror}, device_id_type=MESH,
        )

    def exchange(src, dst, turn):
        far_copy(src, dst, turn).start()
        for e in order:
            @pl.when(inside(e))
            def _():
                near_copy(src, dst, turn, e).start()

    def all_slabs(sem):
        for c in counts:
            @pl.when(count == c)
            def _():
                slabs = recv.at[pl.ds(0, c + 1)]
                pltpu.make_async_copy(slabs, slabs, sem).wait()

    def cut_of(ref, lo, size):
        return lambda i: ref.at[i, pl.ds(lo, size)]

    step = wide // rows

    tiles = slots // step

    def arrived(s, slot):
        for i, (at, lo, _) in enumerate(pieces):
            if (at, lo) == (s, slot):
                load_of(i).wait()
                if i + AHEAD < len(pieces):
                    load_of(i + AHEAD).start()

    def tile_sums(s, accs, todo):
        for t in todo:
            arrived(s, t * step)
            his, los = zip(*[split(land[s, t * step + k]) for k in range(step)])
            rhs = jnp.concatenate(
                [jnp.concatenate(his, axis=0), jnp.concatenate(los, axis=0)], axis=1
            )
            push(rhs, t % 2, t // 2 % 2, transpose=True)
            pltpu.matmul_acc_lhs(accs[t], w_two, load_staged_rhs=t // 2 % 2)

    def cell_sums(sp, accs, cells):
        outs = []
        for acc in accs:
            got = pltpu.matmul_pop(acc)[:parts]
            outs += [got[:, k * rows:(k + 1) * rows] for k in range(step)]
        dose = jnp.concatenate(outs, axis=0)
        onto = one_hot(row_code == keys[sp])
        d1 = dose.astype(BF16)
        rest = dose - d1.astype(F32)
        d2, d3 = split(rest)
        push(jnp.concatenate([d1, d2], axis=1), 0)
        push(lanes_of(d3, wide), 1)
        for cell in cells:
            pltpu.matmul_acc_lhs(cell, onto, load_staged_rhs=0)

    def keep_cells(sp, cells):
        both, third = [pltpu.matmul_pop(cell) for cell in cells]
        total = both[:, :rows] + (both[:, rows:] + third[:, :rows])
        part[:, sp] = total.reshape(dests, 8, rows)

    early = pairs - 1

    def forward(*accs):
        cells, accs = accs[:2], accs[2:]
        sets = [accs[k * two * tiles:(k + 1) * two * tiles] for k in range(2)]
        for s in range(scen):
            sp, s2 = divmod(s, two)
            accs = sets[sp % 2][s2 * tiles:(s2 + 1) * tiles]
            if s2 == 0 and sp:
                tile_sums(s, accs, range(tiles // 2))
                cell_sums(sp - 1, sets[(sp - 1) % 2], cells)
                tile_sums(s, accs, range(tiles // 2, tiles))
                keep_cells(sp - 1, cells)
                if sp == early:
                    pl.semaphore_wait(barrier, count + 1)
                    exchange(cut_of(part, 0, early), cut_of(recv, 0, early), 0)
            else:
                tile_sums(s, accs, range(tiles))
        cell_sums(early, sets[early % 2], cells)
        keep_cells(early, cells)

    pl.run_scoped(
        forward,
        *[pltpu.ACC(u)((qrows, wide), F32) for u in range(2)],
        *[pltpu.ACC(t % 2)((2 * parts, wide), F32) for t in range(2 * two * tiles)],
    )
    exchange(cut_of(part, early, 1), cut_of(recv, early, 1), 0)

    def keep(s, carry):
        for b in range(slots):
            hi, lo = split(land[s, b])
            ihi[s, pl.ds(b * rows, rows)] = hi
            ilo[s, pl.ds(b * rows, rows)] = lo
        return carry

    lax.fori_loop(0, scen, keep, 0)

    lane = iota((width, 2 * 128), 1)
    line = iota((width, 2 * 128), 0)
    q = lane % 128
    lane_code = jnp.where(
        jnp.logical_and(lane // 128 == (line % parts) // sb, q < qrows), rel_of(q), -1000
    )
    for s in range(scen):
        pick[s] = one_hot(key_t[:, s:s + 1] + far * (s % two) == lane_code)
    for load in small[3:]:
        load.wait()
    labels = lab_ref[...]
    target = jnp.zeros(labels.shape, F32)
    for k in range(presc_ref.shape[0]):
        target = jnp.where(labels == k, presc_ref[k], target)
    target = jnp.concatenate([target] * two, axis=0)
    imp = jnp.concatenate([imp_ref[...]] * two, axis=0)

    all_slabs(came.at[0])
    field = part[REACH]
    for i in range(dests):
        if i != REACH:
            field = field + recv[i]
    excess = field - target[None]
    score = imp[None] * excess * excess
    top = jnp.max(score, axis=0)
    top = jnp.maximum(top, pltpu.roll(top, vr, 0))
    expo = jnp.exp(score - top[None])
    whole = jnp.sum(expo, axis=0)
    whole = whole + pltpu.roll(whole, vr, 0)
    coef_now = expo / whole[None] * 2.0 * imp[None] * excess
    coef[...] = coef_now
    exchange(lambda i: coef, lambda i: cbuf.at[i], 1)
    out_ref[pl.ds(0, vr)] = (top + jnp.log(whole))[:vr]
    cbuf[REACH] = coef_now
    all_slabs(sent.at[0])

    all_slabs(came.at[1])
    pad = jnp.zeros((128 - qrows, rows), BF16)

    def picked(*accs):
        for sp in range(pairs):
            c_hi, c_lo = split(cbuf[:, sp].reshape(qrows, rows))
            c_two = jnp.concatenate([c_hi, pad, c_lo, pad], axis=0)
            push(lanes_of(c_two, wide), sp % 2, sp // 2)
            for s2 in range(two):
                pltpu.matmul_acc_lhs(
                    accs[sp * two + s2], pick[sp * two + s2],
                    **({"load_staged_rhs": sp // 2} if s2 == 0 else {}),
                )
        return [pltpu.matmul_pop(acc)[:, :rows] for acc in accs]

    lefts = pl.run_scoped(
        picked, *[pltpu.ACC(s // two % 2)((width, wide), F32) for s in range(scen)]
    )

    def gather(*sums):
        for t in range(scen * slots // step):
            s, b = divmod(t * step, slots)
            unit, stage = t % 2, t // 2 % 2
            block = pl.ds(b * rows, step * rows)
            push(jnp.concatenate([ihi[s, block], ilo[s, block]], axis=1), unit, stage)
            left = jnp.concatenate(
                [lefts[s][(b + k) * parts:(b + k + 1) * parts] for k in range(step)], axis=1
            )
            pltpu.matmul_acc_lhs(
                sums[unit], jnp.concatenate([left, none], axis=0).astype(BF16),
                load_staged_rhs=stage,
            )
        return (pltpu.matmul_pop(sums[0]) + pltpu.matmul_pop(sums[1]))[:parts]

    acc = pl.run_scoped(gather, *[pltpu.ACC(u)((2 * parts, wide), F32) for u in range(2)])
    acc = acc[:, :cols] + acc[:, cols:]
    out_ref[pl.ds(vr, sb)] = acc[:sb] + acc[sb:]

    all_slabs(sent.at[1])


def per_device(influence, spot_weights, vox_block, spot_block, labels, importance, prescription):
    scen, slots, rows, cols = influence.shape
    sb = spot_weights.shape[0] // cols
    vr = labels.shape[0] // rows
    assert 8 % vr == 0 and 2 * vr == 8 and scen % 2 == 0 and 2 * sb == 8
    slab = (scen * vr // 8, 8, rows)
    dests = NEAR + 1
    vmem = pl.BlockSpec(memory_space=pltpu.VMEM)
    both = pl.pallas_call(
        kernel,
        out_shape=pltpu.VMEM((vr + sb, rows), F32),
        in_specs=[pl.BlockSpec(memory_space=pl.ANY)] * 7,
        out_specs=vmem,
        scratch_shapes=[
            pltpu.VMEM((sb, cols), F32),
            pltpu.VMEM(vox_block.shape, jnp.int32),
            pltpu.VMEM(spot_block.shape, jnp.int32),
            pltpu.VMEM((vr, rows), jnp.int32),
            pltpu.VMEM((vr, rows), F32),
            pltpu.SMEM(prescription.shape, F32),
            pltpu.SemaphoreType.DMA((6,)),
            pltpu.VMEM((scen, slots, rows, cols), F32),
            pltpu.VMEM((scen, slots * rows, cols), BF16),
            pltpu.VMEM((scen, slots * rows, cols), BF16),
            pltpu.VMEM((dests,) + slab, F32),
            pltpu.VMEM((dests,) + slab, F32),
            pltpu.VMEM(slab, F32),
            pltpu.VMEM((dests,) + slab, F32),
            pltpu.VMEM((scen, slots * 2 * sb, 256), BF16),
            pltpu.VMEM((scen // 2, 1, 2 * slots * 2 * sb), jnp.int32),
            pltpu.SemaphoreType.DMA((AHEAD,)),
            pltpu.SemaphoreType.DMA((2,)),
            pltpu.SemaphoreType.DMA((2,)),
        ],
        compiler_params=pltpu.CompilerParams(
            collective_id=0, has_side_effects=True, vmem_limit_bytes=56 * 1024 * 1024
        ),
    )(
        influence, spot_weights.reshape(sb, cols), vox_block, spot_block,
        labels.reshape(vr, rows), importance.reshape(vr, rows), prescription,
    )
    return both[:vr].reshape(vr * rows), both[vr:].reshape(sb * cols)


def solution(mesh):
    both = P(("groups", "spots"))
    in_specs = (
        P(None, ("groups", "spots"), None, None),
        both,
        P(None, ("groups", "spots")),
        P(None, ("groups", "spots")),
        both,
        both,
        P("groups"),
    )
    return jax.shard_map(
        per_device, mesh=mesh, in_specs=in_specs, out_specs=(both, both), check_vma=False
    )
```

```python
import jax
import jax.numpy as jnp
from jax import lax
from jax.experimental import pallas as pl
from jax.experimental.pallas import tpu as pltpu
from jax.sharding import PartitionSpec as P

REACH = 4
NEAR = 2 * REACH + 1
AHEAD = 8
STRIP = 16
F32 = jnp.float32
BF16 = jnp.bfloat16
MESH = pl.DeviceIdType.MESH


def split(x):
    hi = x.astype(BF16)
    lo = (x - hi.astype(F32)).astype(BF16)
    return hi, lo


def iota(shape, dim):
    return lax.broadcasted_iota(jnp.int32, shape, dim)


def kernel(
    inf_ref, w_in, vox_in, spot_in, lab_in, imp_in, presc_in,
    out_ref,
    w_ref, vox_ref, spot_ref, lab_ref, imp_ref, presc_ref, small_sem,
    land, ihl, part, recv, coef, cbuf, pick, keys,
    load_sem, sent, came,
):
    scen, slots, rows, cols = land.shape
    vr = lab_ref.shape[0]
    sb = w_ref.shape[0]
    two = 8 // vr
    pairs = scen // two
    dests = NEAR + 1
    qrows = dests * 8
    n = lax.axis_size("spots")
    me = lax.axis_index("spots")
    mirror = lax.rem(me + n // 2, n)

    pieces = [(0, 0, slots // 4), (0, slots // 4, slots - slots // 4)]
    pieces += [(s, h * slots // 2, slots // 2) for s in range(1, scen - 1) for h in range(2)]
    pieces += [(scen - 1, 0, slots // 2), (scen - 1, slots // 2, slots // 2)]

    def load_of(i):
        s, lo, size = pieces[i]
        block = (s, pl.ds(lo, size))
        return pltpu.make_async_copy(inf_ref.at[block], land.at[block], load_sem.at[i % AHEAD])

    small = [
        pltpu.make_async_copy(src, dst, small_sem.at[i])
        for i, (src, dst) in enumerate((
            (w_in, w_ref), (vox_in, vox_ref), (spot_in, spot_ref),
            (lab_in, lab_ref), (imp_in, imp_ref), (presc_in, presc_ref),
        ))
    ]
    for load in small[:3] + [load_of(s) for s in range(AHEAD)] + small[3:]:
        load.start()

    near = [e for e in range(-REACH, REACH + 1) if e != 0]
    order = sorted(near, key=lambda e: (-abs(e), e))

    def inside(e):
        return me + e >= 0 if e < 0 else me + e < n

    barrier = pltpu.get_barrier_semaphore()
    for e in near:
        @pl.when(inside(e))
        def _():
            pl.semaphore_signal(barrier, inc=1, device_id={"spots": me + e}, device_id_type=MESH)
    pl.semaphore_signal(barrier, inc=1, device_id={"spots": mirror}, device_id_type=MESH)

    for e in near:
        @pl.when(jnp.logical_not(inside(e)))
        def _():
            recv[e + REACH] = jnp.zeros(recv.shape[1:], F32)
            cbuf[e + REACH] = jnp.zeros(cbuf.shape[1:], F32)

    small[0].wait()
    w_hi, w_lo = split(w_ref[...])
    w_rows = jnp.concatenate([w_hi.astype(F32), w_lo.astype(F32)], axis=0)
    parts = w_rows.shape[0]
    wide = 2 * cols
    none = jnp.zeros((parts, wide), F32)
    w_two = jnp.concatenate(
        [jnp.concatenate([w_rows, w_rows], axis=1), none], axis=0
    ).astype(BF16)
    width = slots * parts

    def one_hot(mask):
        return mask.astype(F32).astype(BF16)

    def push(rhs, unit, stage=0, transpose=False):
        pltpu.matmul_push_rhs(rhs, stage, unit, transpose=transpose)

    def rows_of(x, count):
        return jnp.concatenate([x, jnp.zeros((count - x.shape[0], x.shape[1]), x.dtype)], axis=0)

    def lanes_of(x, count):
        return jnp.concatenate([x, jnp.zeros((x.shape[0], count - x.shape[1]), x.dtype)], axis=1)

    far = sb * vr * dests * 2

    def rel_of(q):
        return sb * ((q // 8) * vr + q % vr) + far * ((q % 8) // vr)

    count = sum(inside(e).astype(jnp.int32) for e in near)
    counts = sorted({sum(0 <= m + e < n for e in near) for m in range(n)})

    def near_copy(src, dst, turn, e):
        return pltpu.make_async_remote_copy(
            src_ref=src(REACH + e), dst_ref=dst(REACH - e),
            send_sem=sent.at[turn], recv_sem=came.at[turn],
            device_id={"spots": me + e}, device_id_type=MESH,
        )

    def far_copy(src, dst, turn):
        return pltpu.make_async_remote_copy(
            src_ref=src(NEAR), dst_ref=dst(NEAR),
            send_sem=sent.at[turn], recv_sem=came.at[turn],
            device_id={"spots": mirror}, device_id_type=MESH,
        )

    def exchange(src, dst, turn):
        far_copy(src, dst, turn).start()
        for e in order:
            @pl.when(inside(e))
            def _():
                near_copy(src, dst, turn, e).start()

    def all_slabs(sem):
        for c in counts:
            @pl.when(count == c)
            def _():
                slabs = recv.at[pl.ds(0, c + 1)]
                pltpu.make_async_copy(slabs, slabs, sem).wait()

    def cut_of(ref, lo, size):
        return lambda i: ref.at[i, pl.ds(lo, size)]

    def place_slots():
        small[1].wait()
        small[2].wait()
        vox = vox_ref[...]
        slot_id = iota(vox.shape, 1)
        rel = jnp.where(
            slot_id == 0,
            vox - vr * mirror + vr * NEAR,
            vox - vr * me + vr * REACH,
        )
        code = rows_of(lanes_of((rel * sb + spot_ref[...]).astype(F32), wide), wide).astype(BF16)

        def codes(acc, acc_t):
            push(one_hot(iota((wide, wide), 1) // parts == iota((wide, wide), 0)), 0)
            pltpu.matmul_acc_lhs(acc, code[:2 * scen], load_staged_rhs=0)
            push(code, 1, transpose=True)
            pltpu.matmul_acc_lhs(
                acc_t, one_hot(iota((width, wide), 0) // parts == iota((width, wide), 1)),
                load_staged_rhs=0,
            )
            return pltpu.matmul_pop(acc)[:scen, :width], pltpu.matmul_pop(acc_t)[:, :cols]

        key, key_t = pl.run_scoped(
            codes, pltpu.ACC(0)((2 * scen, wide), F32), pltpu.ACC(1)((width, wide), F32)
        )
        key = key.astype(jnp.int32) - iota((scen, width), 1) % sb
        key_t = key_t.astype(jnp.int32) - iota((width, cols), 0) % sb

        row_code = rel_of(iota((qrows, two * width), 0))
        for sp in range(pairs):
            keys[sp] = jnp.concatenate(
                [key[sp * two + s2:sp * two + s2 + 1] + far * s2 for s2 in range(two)], axis=1
            )

        return key_t, row_code

    step = wide // rows

    tiles = slots // step

    def arrived(s, slot):
        for i, (at, lo, _) in enumerate(pieces):
            if (at, lo) == (s, slot):
                load_of(i).wait()
                if i + AHEAD < len(pieces):
                    load_of(i + AHEAD).start()

    def tile_sums(s, accs, todo):
        for t in todo:
            arrived(s, t * step)
            his, los = zip(*[split(land[s, t * step + k]) for k in range(step)])
            rhs = jnp.concatenate(
                [jnp.concatenate(his, axis=0), jnp.concatenate(los, axis=0)], axis=1
            )
            push(rhs, t % 2, t // 2 % 2, transpose=True)
            pltpu.matmul_acc_lhs(accs[t], w_two, load_staged_rhs=t // 2 % 2)

    def cell_sums(sp, accs, cells, row_code):
        outs = []
        for acc in accs:
            got = pltpu.matmul_pop(acc)[:parts]
            outs += [got[:, k * rows:(k + 1) * rows] for k in range(step)]
        dose = jnp.concatenate(outs, axis=0)
        onto = one_hot(row_code == keys[sp])
        d1 = dose.astype(BF16)
        rest = dose - d1.astype(F32)
        d2, d3 = split(rest)
        push(jnp.concatenate([d1, d2], axis=1), 0)
        push(lanes_of(d3, wide), 1)
        for cell in cells:
            pltpu.matmul_acc_lhs(cell, onto, load_staged_rhs=0)

    def keep_cells(sp, cells):
        both, third = [pltpu.matmul_pop(cell) for cell in cells]
        total = both[:, :rows] + (both[:, rows:] + third[:, :rows])
        part[:, sp] = total.reshape(dests, 8, rows)

    early = pairs - 1

    def forward(*accs):
        cells, accs = accs[:2], accs[2:]
        sets = [accs[k * two * tiles:(k + 1) * two * tiles] for k in range(2)]
        for s in range(scen):
            sp, s2 = divmod(s, two)
            accs = sets[sp % 2][s2 * tiles:(s2 + 1) * tiles]
            if s2 == 0 and sp:
                tile_sums(s, accs, range(tiles // 2))
                cell_sums(sp - 1, sets[(sp - 1) % 2], cells, row_code)
                tile_sums(s, accs, range(tiles // 2, tiles))
                keep_cells(sp - 1, cells)
                if sp == 2:
                    pl.semaphore_wait(barrier, count + 1)
                    exchange(cut_of(part, 0, 2), cut_of(recv, 0, 2), 0)
                if sp == 3:
                    exchange(cut_of(part, 2, 1), cut_of(recv, 2, 1), 0)
            else:
                tile_sums(s, accs, range(tiles))
            if s == 0:
                key_t, row_code = place_slots()
        cell_sums(early, sets[early % 2], cells, row_code)
        keep_cells(early, cells)
        return key_t

    key_t = pl.run_scoped(
        forward,
        *[pltpu.ACC(u)((qrows, wide), F32) for u in range(2)],
        *[pltpu.ACC(t % 2)((2 * parts, wide), F32) for t in range(2 * two * tiles)],
    )
    exchange(cut_of(part, early, 1), cut_of(recv, early, 1), 0)

    def keep(s, carry):
        for b in range(slots):
            hi, lo = split(land[s, b])
            strips = pl.ds(b * (rows // STRIP), rows // STRIP)
            ihl[s, strips, 0] = hi.reshape(rows // STRIP, STRIP, cols)
            ihl[s, strips, 1] = lo.reshape(rows // STRIP, STRIP, cols)
        return carry

    lax.fori_loop(0, scen, keep, 0)

    lane = iota((width, 2 * 128), 1)
    line = iota((width, 2 * 128), 0)
    q = lane % 128
    lane_code = jnp.where(
        jnp.logical_and(lane // 128 == (line % parts) // sb, q < qrows), rel_of(q), -1000
    )
    for s in range(scen):
        pick[s] = one_hot(key_t[:, s:s + 1] + far * (s % two) == lane_code)
    for load in small[3:]:
        load.wait()
    labels = lab_ref[...]
    target = jnp.zeros(labels.shape, F32)
    for k in range(presc_ref.shape[0]):
        target = jnp.where(labels == k, presc_ref[k], target)
    target = jnp.concatenate([target] * two, axis=0)
    imp = jnp.concatenate([imp_ref[...]] * two, axis=0)

    all_slabs(came.at[0])
    field = part[REACH]
    for i in range(dests):
        if i != REACH:
            field = field + recv[i]
    excess = field - target[None]
    score = imp[None] * excess * excess
    top = jnp.max(score, axis=0)
    top = jnp.maximum(top, pltpu.roll(top, vr, 0))
    expo = jnp.exp(score - top[None])
    whole = jnp.sum(expo, axis=0)
    whole = whole + pltpu.roll(whole, vr, 0)
    coef_now = expo / whole[None] * 2.0 * imp[None] * excess
    coef[...] = coef_now
    exchange(lambda i: coef, lambda i: cbuf.at[i], 1)
    out_ref[pl.ds(0, vr)] = (top + jnp.log(whole))[:vr]
    cbuf[REACH] = coef_now
    all_slabs(sent.at[0])

    all_slabs(came.at[1])
    pad = jnp.zeros((128 - qrows, rows), BF16)

    def picked(*accs):
        for sp in range(pairs):
            c_hi, c_lo = split(cbuf[:, sp].reshape(qrows, rows))
            c_two = jnp.concatenate([c_hi, pad, c_lo, pad], axis=0)
            push(lanes_of(c_two, wide), sp % 2, sp // 2)
            for s2 in range(two):
                pltpu.matmul_acc_lhs(
                    accs[sp * two + s2], pick[sp * two + s2],
                    **({"load_staged_rhs": sp // 2} if s2 == 0 else {}),
                )
        return [pltpu.matmul_pop(acc)[:, :rows] for acc in accs]

    lefts = pl.run_scoped(
        picked, *[pltpu.ACC(s // two % 2)((width, wide), F32) for s in range(scen)]
    )

    def gather(*sums):
        for t in range(scen * slots // step):
            s, b = divmod(t * step, slots)
            unit, stage = t % 2, t // 2 % 2
            strips = pl.ds(b * (rows // STRIP), step * (rows // STRIP))
            push(
                jnp.concatenate(
                    [ihl[s, strips, h].reshape(step * rows, cols) for h in range(2)], axis=1
                ), unit, stage,
            )
            left = jnp.concatenate(
                [lefts[s][(b + k) * parts:(b + k + 1) * parts] for k in range(step)], axis=1
            )
            pltpu.matmul_acc_lhs(
                sums[unit], jnp.concatenate([left, none], axis=0).astype(BF16),
                load_staged_rhs=stage,
            )
        return (pltpu.matmul_pop(sums[0]) + pltpu.matmul_pop(sums[1]))[:parts]

    acc = pl.run_scoped(gather, *[pltpu.ACC(u)((2 * parts, wide), F32) for u in range(2)])
    acc = acc[:, :cols] + acc[:, cols:]
    out_ref[pl.ds(vr, sb)] = acc[:sb] + acc[sb:]

    all_slabs(sent.at[1])


def per_device(influence, spot_weights, vox_block, spot_block, labels, importance, prescription):
    scen, slots, rows, cols = influence.shape
    sb = spot_weights.shape[0] // cols
    vr = labels.shape[0] // rows
    assert 8 % vr == 0 and 2 * vr == 8 and scen % 2 == 0 and 2 * sb == 8
    slab = (scen * vr // 8, 8, rows)
    dests = NEAR + 1
    vmem = pl.BlockSpec(memory_space=pltpu.VMEM)
    both = pl.pallas_call(
        kernel,
        out_shape=pltpu.VMEM((vr + sb, rows), F32),
        in_specs=[pl.BlockSpec(memory_space=pl.ANY)] * 7,
        out_specs=vmem,
        scratch_shapes=[
            pltpu.VMEM((sb, cols), F32),
            pltpu.VMEM(vox_block.shape, jnp.int32),
            pltpu.VMEM(spot_block.shape, jnp.int32),
            pltpu.VMEM((vr, rows), jnp.int32),
            pltpu.VMEM((vr, rows), F32),
            pltpu.SMEM(prescription.shape, F32),
            pltpu.SemaphoreType.DMA((6,)),
            pltpu.VMEM((scen, slots, rows, cols), F32),
            pltpu.VMEM((scen, slots * rows // STRIP, 2, STRIP, cols), BF16),
            pltpu.VMEM((dests,) + slab, F32),
            pltpu.VMEM((dests,) + slab, F32),
            pltpu.VMEM(slab, F32),
            pltpu.VMEM((dests,) + slab, F32),
            pltpu.VMEM((scen, slots * 2 * sb, 256), BF16),
            pltpu.VMEM((scen // 2, 1, 2 * slots * 2 * sb), jnp.int32),
            pltpu.SemaphoreType.DMA((AHEAD,)),
            pltpu.SemaphoreType.DMA((2,)),
            pltpu.SemaphoreType.DMA((2,)),
        ],
        compiler_params=pltpu.CompilerParams(
            collective_id=0, has_side_effects=True, vmem_limit_bytes=56 * 1024 * 1024
        ),
    )(
        influence, spot_weights.reshape(sb, cols), vox_block, spot_block,
        labels.reshape(vr, rows), importance.reshape(vr, rows), prescription,
    )
    return both[:vr].reshape(vr * rows), both[vr:].reshape(sb * cols)


def solution(mesh):
    both = P(("groups", "spots"))
    in_specs = (
        P(None, ("groups", "spots"), None, None),
        both,
        P(None, ("groups", "spots")),
        P(None, ("groups", "spots")),
        both,
        both,
        P("groups"),
    )
    return jax.shard_map(
        per_device, mesh=mesh, in_specs=in_specs, out_specs=(both, both), check_vma=False
    )
```

```python
import jax
import jax.numpy as jnp
from jax import lax
from jax.experimental import pallas as pl
from jax.experimental.pallas import tpu as pltpu
from jax.sharding import PartitionSpec as P

REACH = 4
NEAR = 2 * REACH + 1
AHEAD = 8
STRIP = 16
BY_ROWS = 2
F32 = jnp.float32
BF16 = jnp.bfloat16
MESH = pl.DeviceIdType.MESH


def split(x):
    hi = x.astype(BF16)
    lo = (x - hi.astype(F32)).astype(BF16)
    return hi, lo


def iota(shape, dim):
    return lax.broadcasted_iota(jnp.int32, shape, dim)


def kernel(*refs):
    pl.run_scoped(
        lambda *sems: plan(*refs, *sems),
        pltpu.SemaphoreType.DMA((6,)), pltpu.SemaphoreType.DMA((AHEAD,)),
    )


def plan(
    inf_ref, w_in, vox_in, spot_in, lab_in, imp_in, presc_in,
    out_ref,
    w_ref, vox_ref, spot_ref, lab_ref, imp_ref, presc_ref,
    land, ihl, part, recv, coef, cbuf, pick, keys, spot_rows,
    sent, came, small_sem, load_sem,
):
    scen, slots, rows, cols = land.shape
    vr = lab_ref.shape[0]
    sb = w_ref.shape[0]
    two = 8 // vr
    pairs = scen // two
    dests = NEAR + 1
    qrows = dests * 8
    n = lax.axis_size("spots")
    me = lax.axis_index("spots")
    mirror = lax.rem(me + n // 2, n)

    pieces = [(0, 0, slots // 4), (0, slots // 4, slots - slots // 4)]
    pieces += [(s, h * slots // 2, slots // 2) for s in range(1, scen - 1) for h in range(2)]
    pieces += [(scen - 1, 0, slots // 2), (scen - 1, slots // 2, slots // 2)]

    def load_of(i):
        s, lo, size = pieces[i]
        block = (s, pl.ds(lo, size))
        return pltpu.make_async_copy(inf_ref.at[block], land.at[block], load_sem.at[i % AHEAD])

    small = [
        pltpu.make_async_copy(src, dst, small_sem.at[i])
        for i, (src, dst) in enumerate((
            (w_in, w_ref), (vox_in, vox_ref), (spot_in, spot_ref),
            (lab_in, lab_ref), (imp_in, imp_ref), (presc_in, presc_ref),
        ))
    ]
    for load in small[:3] + [load_of(s) for s in range(AHEAD)] + small[3:]:
        load.start()

    near = [e for e in range(-REACH, REACH + 1) if e != 0]
    order = sorted(near, key=lambda e: (-abs(e), e))

    def inside(e):
        return me + e >= 0 if e < 0 else me + e < n

    barrier = pltpu.get_barrier_semaphore()
    for e in near:
        @pl.when(inside(e))
        def _():
            pl.semaphore_signal(barrier, inc=1, device_id={"spots": me + e}, device_id_type=MESH)
    pl.semaphore_signal(barrier, inc=1, device_id={"spots": mirror}, device_id_type=MESH)

    for e in near:
        @pl.when(jnp.logical_not(inside(e)))
        def _():
            recv[e + REACH] = jnp.zeros(recv.shape[1:], F32)
            cbuf[e + REACH] = jnp.zeros(cbuf.shape[1:], F32)

    small[0].wait()
    w_hi, w_lo = split(w_ref[...])
    w_rows = jnp.concatenate([w_hi.astype(F32), w_lo.astype(F32)], axis=0)
    parts = w_rows.shape[0]
    wide = 2 * cols
    none = jnp.zeros((parts, wide), F32)
    w_two = jnp.concatenate(
        [jnp.concatenate([w_rows, w_rows], axis=1), none], axis=0
    ).astype(BF16)
    width = slots * parts

    def one_hot(mask):
        return mask.astype(F32).astype(BF16)

    def push(rhs, unit, stage=0, transpose=False):
        pltpu.matmul_push_rhs(rhs, stage, unit, transpose=transpose)

    def rows_of(x, count):
        return jnp.concatenate([x, jnp.zeros((count - x.shape[0], x.shape[1]), x.dtype)], axis=0)

    def lanes_of(x, count):
        return jnp.concatenate([x, jnp.zeros((x.shape[0], count - x.shape[1]), x.dtype)], axis=1)

    far = sb * vr * dests * 2

    def rel_of(q):
        return sb * ((q // 8) * vr + q % vr) + far * ((q % 8) // vr)

    count = sum(inside(e).astype(jnp.int32) for e in near)
    counts = sorted({sum(0 <= m + e < n for e in near) for m in range(n)})

    def near_copy(src, dst, turn, e):
        return pltpu.make_async_remote_copy(
            src_ref=src(REACH + e), dst_ref=dst(REACH - e),
            send_sem=sent.at[turn], recv_sem=came.at[turn],
            device_id={"spots": me + e}, device_id_type=MESH,
        )

    def far_copy(src, dst, turn):
        return pltpu.make_async_remote_copy(
            src_ref=src(NEAR), dst_ref=dst(NEAR),
            send_sem=sent.at[turn], recv_sem=came.at[turn],
            device_id={"spots": mirror}, device_id_type=MESH,
        )

    def exchange(src, dst, turn):
        far_copy(src, dst, turn).start()
        for e in order:
            @pl.when(inside(e))
            def _():
                near_copy(src, dst, turn, e).start()

    def all_slabs(sem):
        for c in counts:
            @pl.when(count == c)
            def _():
                slabs = recv.at[pl.ds(0, c + 1)]
                pltpu.make_async_copy(slabs, slabs, sem).wait()

    def cut_of(ref, lo, size):
        return lambda i: ref.at[i, pl.ds(lo, size)]

    def place_slots():
        small[1].wait()
        small[2].wait()
        vox = vox_ref[...]
        slot_id = iota(vox.shape, 1)
        rel = jnp.where(
            slot_id == 0,
            vox - vr * mirror + vr * NEAR,
            vox - vr * me + vr * REACH,
        )
        code = rows_of(lanes_of((rel * sb + spot_ref[...]).astype(F32), wide), wide).astype(BF16)

        def codes(acc, acc_t):
            push(one_hot(iota((wide, wide), 1) // parts == iota((wide, wide), 0)), 0)
            pltpu.matmul_acc_lhs(acc, code[:2 * scen], load_staged_rhs=0)
            push(code, 1, transpose=True)
            pltpu.matmul_acc_lhs(
                acc_t, one_hot(iota((width, wide), 0) // parts == iota((width, wide), 1)),
                load_staged_rhs=0,
            )
            return pltpu.matmul_pop(acc)[:scen, :width], pltpu.matmul_pop(acc_t)[:, :cols]

        key, key_t = pl.run_scoped(
            codes, pltpu.ACC(0)((2 * scen, wide), F32), pltpu.ACC(1)((width, wide), F32)
        )
        key = key.astype(jnp.int32) - iota((scen, width), 1) % sb
        key_t = key_t.astype(jnp.int32) - iota((width, cols), 0) % sb

        row_code = rel_of(iota((qrows, two * width), 0))
        for sp in range(pairs):
            keys[sp] = jnp.concatenate(
                [key[sp * two + s2:sp * two + s2 + 1] + far * s2 for s2 in range(two)], axis=1
            )

        return key_t, row_code

    step = wide // rows

    tiles = slots // step

    def arrived(s, slot):
        for i, (at, lo, _) in enumerate(pieces):
            if (at, lo) == (s, slot):
                load_of(i).wait()
                if i + AHEAD < len(pieces):
                    load_of(i + AHEAD).start()

    def tile_sums(s, accs, todo):
        for t in todo:
            arrived(s, t * step)
            his, los = zip(*[split(land[s, t * step + k]) for k in range(step)])
            rhs = jnp.concatenate(
                [jnp.concatenate(his, axis=0), jnp.concatenate(los, axis=0)], axis=1
            )
            push(rhs, t % 2, t // 2 % 2, transpose=True)
            pltpu.matmul_acc_lhs(accs[t], w_two, load_staged_rhs=t // 2 % 2)

    def cell_sums(sp, accs, cells, row_code):
        outs = []
        for acc in accs:
            got = pltpu.matmul_pop(acc)[:parts]
            outs += [got[:, k * rows:(k + 1) * rows] for k in range(step)]
        dose = jnp.concatenate(outs, axis=0)
        onto = one_hot(row_code == keys[sp])
        d1 = dose.astype(BF16)
        rest = dose - d1.astype(F32)
        d2, d3 = split(rest)
        push(jnp.concatenate([d1, d2], axis=1), 0)
        push(lanes_of(d3, wide), 1)
        for cell in cells:
            pltpu.matmul_acc_lhs(cell, onto, load_staged_rhs=0)

    def keep_cells(sp, cells):
        both, third = [pltpu.matmul_pop(cell) for cell in cells]
        total = both[:, :rows] + (both[:, rows:] + third[:, :rows])
        part[:, sp] = total.reshape(dests, 8, rows)

    early = pairs - 1

    def forward(*accs):
        cells, accs = accs[:2], accs[2:]
        sets = [accs[k * two * tiles:(k + 1) * two * tiles] for k in range(2)]
        for s in range(scen):
            sp, s2 = divmod(s, two)
            accs = sets[sp % 2][s2 * tiles:(s2 + 1) * tiles]
            if s2 == 0 and sp:
                tile_sums(s, accs, range(tiles // 2))
                cell_sums(sp - 1, sets[(sp - 1) % 2], cells, row_code)
                tile_sums(s, accs, range(tiles // 2, tiles))
                keep_cells(sp - 1, cells)
                if sp == 2:
                    pl.semaphore_wait(barrier, count + 1)
                    exchange(cut_of(part, 0, 2), cut_of(recv, 0, 2), 0)
                if sp == 3:
                    exchange(cut_of(part, 2, 1), cut_of(recv, 2, 1), 0)
            else:
                tile_sums(s, accs, range(tiles))
            if s == 0:
                key_t, row_code = place_slots()
        cell_sums(early, sets[early % 2], cells, row_code)
        keep_cells(early, cells)
        return key_t

    key_t = pl.run_scoped(
        forward,
        *[pltpu.ACC(u)((qrows, wide), F32) for u in range(2)],
        *[pltpu.ACC(t % 2)((2 * parts, wide), F32) for t in range(2 * two * tiles)],
    )
    exchange(cut_of(part, early, 1), cut_of(recv, early, 1), 0)

    pushed = slots - BY_ROWS

    def keep(s, carry):
        for b in range(pushed):
            hi, lo = split(land[s, b])
            strips = pl.ds(b * (rows // STRIP), rows // STRIP)
            ihl[s, strips, 0] = hi.reshape(rows // STRIP, STRIP, cols)
            ihl[s, strips, 1] = lo.reshape(rows // STRIP, STRIP, cols)
        return carry

    lax.fori_loop(0, scen, keep, 0)

    lane = iota((width, 2 * 128), 1)
    line = iota((width, 2 * 128), 0)
    q = lane % 128
    lane_code = jnp.where(
        jnp.logical_and(lane // 128 == (line % parts) // sb, q < qrows), rel_of(q), -1000
    )
    for s in range(scen):
        pick[s] = one_hot(key_t[:, s:s + 1] + far * (s % two) == lane_code)
    line = iota((parts, rows), 0)
    for s in range(scen):
        for k in range(BY_ROWS):
            at = (pushed + k) * parts
            own = jnp.broadcast_to(lax.rem(key_t[at:at + parts, s:s + 1], sb), line.shape) == 0
            spot_rows[s * BY_ROWS + k] = jnp.where(jnp.logical_and(own, line < sb), 1.0, 0.0)
    for load in small[3:]:
        load.wait()
    labels = lab_ref[...]
    target = jnp.zeros(labels.shape, F32)
    for k in range(presc_ref.shape[0]):
        target = jnp.where(labels == k, presc_ref[k], target)
    target = jnp.concatenate([target] * two, axis=0)
    imp = jnp.concatenate([imp_ref[...]] * two, axis=0)

    all_slabs(came.at[0])
    field = part[REACH]
    for i in range(dests):
        if i != REACH:
            field = field + recv[i]
    excess = field - target[None]
    score = imp[None] * excess * excess
    top = jnp.max(score, axis=0)
    top = jnp.maximum(top, pltpu.roll(top, vr, 0))
    expo = jnp.exp(score - top[None])
    whole = jnp.sum(expo, axis=0)
    whole = whole + pltpu.roll(whole, vr, 0)
    coef_now = expo / whole[None] * 2.0 * imp[None] * excess
    coef[...] = coef_now
    exchange(lambda i: coef, lambda i: cbuf.at[i], 1)
    out_ref[pl.ds(0, vr)] = (top + jnp.log(whole))[:vr]
    cbuf[REACH] = coef_now
    all_slabs(sent.at[0])

    all_slabs(came.at[1])
    pad = jnp.zeros((128 - qrows, rows), BF16)

    def picked(*accs):
        for sp in range(pairs):
            c_hi, c_lo = split(cbuf[:, sp].reshape(qrows, rows))
            c_two = jnp.concatenate([c_hi, pad, c_lo, pad], axis=0)
            push(lanes_of(c_two, wide), sp % 2, sp // 2)
            for s2 in range(two):
                pltpu.matmul_acc_lhs(
                    accs[sp * two + s2], pick[sp * two + s2],
                    **({"load_staged_rhs": sp // 2} if s2 == 0 else {}),
                )
        return [pltpu.matmul_pop(acc)[:, :rows] for acc in accs]

    lefts = pl.run_scoped(
        picked, *[pltpu.ACC(s // two % 2)((width, wide), F32) for s in range(scen)]
    )

    coef_rows = jnp.concatenate(
        [
            jnp.sum(lefts[s][b * parts:(b + 1) * parts], axis=0, keepdims=True)
            for s in range(scen) for b in range(pushed, slots)
        ], axis=0,
    )
    coef_cols = rows_of(coef_rows, rows).T

    def by_rows(v):
        s, k = divmod(v, BY_ROWS)
        prod = land[s, pushed + k] * coef_cols[:, v:v + 1]
        tall = jnp.sum(prod.reshape(rows // 8, 8, cols), axis=0)
        return spot_rows[v] * jnp.sum(tall, axis=0, keepdims=True)

    def gather(*sums):
        count_t, count_v, done, rest = scen * pushed // step, scen * BY_ROWS, 0, 0.0
        for t in range(count_t):
            while done < count_v and (done + 1) * (count_t - 8) <= (t + 1 - 8) * count_v:
                rest = rest + by_rows(done)
                done += 1
            s, b = divmod(t * step, pushed)
            unit, stage = t % 2, t // 2 % 2
            strips = pl.ds(b * (rows // STRIP), step * (rows // STRIP))
            push(
                jnp.concatenate(
                    [ihl[s, strips, h].reshape(step * rows, cols) for h in range(2)], axis=1
                ), unit, stage,
            )
            left = jnp.concatenate(
                [lefts[s][(b + k) * parts:(b + k + 1) * parts] for k in range(step)], axis=1
            )
            pltpu.matmul_acc_lhs(
                sums[unit], jnp.concatenate([left, none], axis=0).astype(BF16),
                load_staged_rhs=stage,
            )
        return (pltpu.matmul_pop(sums[0]) + pltpu.matmul_pop(sums[1]))[:parts], rest

    acc, rest = pl.run_scoped(gather, *[pltpu.ACC(u)((2 * parts, wide), F32) for u in range(2)])
    acc = acc[:, :cols] + acc[:, cols:]
    acc = acc + rest
    out_ref[pl.ds(vr, sb)] = acc[:sb] + acc[sb:]

    all_slabs(sent.at[1])


def per_device(influence, spot_weights, vox_block, spot_block, labels, importance, prescription):
    scen, slots, rows, cols = influence.shape
    sb = spot_weights.shape[0] // cols
    vr = labels.shape[0] // rows
    assert 8 % vr == 0 and 2 * vr == 8 and scen % 2 == 0 and 2 * sb == 8
    slab = (scen * vr // 8, 8, rows)
    dests = NEAR + 1
    vmem = pl.BlockSpec(memory_space=pltpu.VMEM)
    both = pl.pallas_call(
        kernel,
        out_shape=pltpu.VMEM((vr + sb, rows), F32),
        in_specs=[pl.BlockSpec(memory_space=pl.ANY)] * 7,
        out_specs=vmem,
        scratch_shapes=[
            pltpu.VMEM((sb, cols), F32),
            pltpu.VMEM(vox_block.shape, jnp.int32),
            pltpu.VMEM(spot_block.shape, jnp.int32),
            pltpu.VMEM((vr, rows), jnp.int32),
            pltpu.VMEM((vr, rows), F32),
            pltpu.SMEM(prescription.shape, F32),
            pltpu.VMEM((scen, slots, rows, cols), F32),
            pltpu.VMEM((scen, slots * rows // STRIP, 2, STRIP, cols), BF16),
            pltpu.VMEM((dests,) + slab, F32),
            pltpu.VMEM((dests,) + slab, F32),
            pltpu.VMEM(slab, F32),
            pltpu.VMEM((dests,) + slab, F32),
            pltpu.VMEM((scen, slots * 2 * sb, 256), BF16),
            pltpu.VMEM((scen // 2, 1, 2 * slots * 2 * sb), jnp.int32),
            pltpu.VMEM((scen * BY_ROWS, 2 * sb, rows), F32),
            pltpu.SemaphoreType.DMA((2,)),
            pltpu.SemaphoreType.DMA((2,)),
        ],
        compiler_params=pltpu.CompilerParams(
            collective_id=0, has_side_effects=True, vmem_limit_bytes=56 * 1024 * 1024
        ),
    )(
        influence, spot_weights.reshape(sb, cols), vox_block, spot_block,
        labels.reshape(vr, rows), importance.reshape(vr, rows), prescription,
    )
    return both[:vr].reshape(vr * rows), both[vr:].reshape(sb * cols)


def solution(mesh):
    both = P(("groups", "spots"))
    in_specs = (
        P(None, ("groups", "spots"), None, None),
        both,
        P(None, ("groups", "spots")),
        P(None, ("groups", "spots")),
        both,
        both,
        P("groups"),
    )
    return jax.shard_map(
        per_device, mesh=mesh, in_specs=in_specs, out_specs=(both, both), check_vma=False
    )
```

```python
import jax
import jax.numpy as jnp
from jax import lax
from jax.experimental import pallas as pl
from jax.experimental.pallas import tpu as pltpu
from jax.sharding import PartitionSpec as P

REACH = 4
NEAR = 2 * REACH + 1
AHEAD = 8
STRIP = 16
BY_ROWS = 2
F32 = jnp.float32
BF16 = jnp.bfloat16
MESH = pl.DeviceIdType.MESH


def split(x):
    hi = x.astype(BF16)
    lo = (x - hi.astype(F32)).astype(BF16)
    return hi, lo


def iota(shape, dim):
    return lax.broadcasted_iota(jnp.int32, shape, dim)


def kernel(*refs):
    pl.run_scoped(
        lambda *sems: plan(*refs, *sems),
        pltpu.SemaphoreType.DMA((6,)), pltpu.SemaphoreType.DMA((AHEAD,)),
    )


def plan(
    inf_ref, w_in, vox_in, spot_in, lab_in, imp_in, presc_in,
    out_ref,
    w_ref, vox_ref, spot_ref, lab_ref, imp_ref, presc_ref,
    land, ihl, part, recv, coef, cbuf, pick, keys, spot_rows,
    far_vox, asked, far_coef, sent, came, small_sem, load_sem,
):
    scen, slots, rows, cols = land.shape
    vr = lab_ref.shape[0]
    sb = w_ref.shape[0]
    two = 8 // vr
    pairs = scen // two
    dests = NEAR + 1
    qrows = dests * 8
    n = lax.axis_size("spots")
    me = lax.axis_index("spots")
    mirror = lax.rem(me + n // 2, n)

    pieces = [(0, 0, slots // 4), (0, slots // 4, slots - slots // 4)]
    pieces += [(s, h * slots // 2, slots // 2) for s in range(1, scen - 1) for h in range(2)]
    pieces += [(scen - 1, 0, slots // 2), (scen - 1, slots // 2, slots // 2)]

    def load_of(i):
        s, lo, size = pieces[i]
        block = (s, pl.ds(lo, size))
        return pltpu.make_async_copy(inf_ref.at[block], land.at[block], load_sem.at[i % AHEAD])

    small = [
        pltpu.make_async_copy(src, dst, small_sem.at[i])
        for i, (src, dst) in enumerate((
            (w_in, w_ref), (vox_in, vox_ref), (spot_in, spot_ref),
            (lab_in, lab_ref), (imp_in, imp_ref), (presc_in, presc_ref),
        ))
    ]
    for load in small[:3] + [load_of(s) for s in range(AHEAD)] + small[3:]:
        load.start()

    near = [e for e in range(-REACH, REACH + 1) if e != 0]
    order = sorted(near, key=lambda e: (-abs(e), e))

    def inside(e):
        return me + e >= 0 if e < 0 else me + e < n

    barrier = pltpu.get_barrier_semaphore()
    for e in near:
        @pl.when(inside(e))
        def _():
            pl.semaphore_signal(barrier, inc=1, device_id={"spots": me + e}, device_id_type=MESH)
    pl.semaphore_signal(barrier, inc=1, device_id={"spots": mirror}, device_id_type=MESH)

    for e in near:
        @pl.when(jnp.logical_not(inside(e)))
        def _():
            recv[e + REACH] = jnp.zeros(recv.shape[1:], F32)
            cbuf[e + REACH] = jnp.zeros(cbuf.shape[1:], F32)

    small[0].wait()
    w_hi, w_lo = split(w_ref[...])
    w_rows = jnp.concatenate([w_hi.astype(F32), w_lo.astype(F32)], axis=0)
    parts = w_rows.shape[0]
    wide = 2 * cols
    none = jnp.zeros((parts, wide), F32)
    w_two = jnp.concatenate(
        [jnp.concatenate([w_rows, w_rows], axis=1), none], axis=0
    ).astype(BF16)
    width = slots * parts

    def one_hot(mask):
        return mask.astype(F32).astype(BF16)

    def push(rhs, unit, stage=0, transpose=False):
        pltpu.matmul_push_rhs(rhs, stage, unit, transpose=transpose)

    def rows_of(x, count):
        return jnp.concatenate([x, jnp.zeros((count - x.shape[0], x.shape[1]), x.dtype)], axis=0)

    def lanes_of(x, count):
        return jnp.concatenate([x, jnp.zeros((x.shape[0], count - x.shape[1]), x.dtype)], axis=1)

    far = sb * vr * dests * 2

    def rel_of(q):
        return sb * ((q // 8) * vr + q % vr) + far * ((q % 8) // vr)

    count = sum(inside(e).astype(jnp.int32) for e in near)
    counts = sorted({sum(0 <= m + e < n for e in near) for m in range(n)})

    def near_copy(src, dst, turn, e):
        return pltpu.make_async_remote_copy(
            src_ref=src(REACH + e), dst_ref=dst(REACH - e),
            send_sem=sent.at[turn], recv_sem=came.at[turn],
            device_id={"spots": me + e}, device_id_type=MESH,
        )

    def far_copy(src, dst, turn):
        return pltpu.make_async_remote_copy(
            src_ref=src(NEAR), dst_ref=dst(NEAR),
            send_sem=sent.at[turn], recv_sem=came.at[turn],
            device_id={"spots": mirror}, device_id_type=MESH,
        )

    def to_mirror(src, dst, turn):
        return pltpu.make_async_remote_copy(
            src_ref=src, dst_ref=dst, send_sem=sent.at[turn], recv_sem=came.at[turn],
            device_id={"spots": mirror}, device_id_type=MESH,
        )

    def exchange(src, dst, turn):
        if turn == 0:
            far_copy(src, dst, turn).start()
        else:
            to_mirror(asked, far_coef, 3).start()
        for e in order:
            @pl.when(inside(e))
            def _():
                near_copy(src, dst, turn, e).start()

    def all_slabs(sem, more=1):
        for c in counts:
            @pl.when(count == c)
            def _():
                slabs = recv.at[pl.ds(0, c + more)]
                pltpu.make_async_copy(slabs, slabs, sem).wait()

    def cut_of(ref, lo, size):
        return lambda i: ref.at[i, pl.ds(lo, size)]

    def place_slots():
        small[1].wait()
        small[2].wait()
        vox = vox_ref[...]
        slot_id = iota(vox.shape, 1)
        rel = jnp.where(
            slot_id == 0,
            vox - vr * mirror + vr * NEAR,
            vox - vr * me + vr * REACH,
        )
        code = rows_of(lanes_of((rel * sb + spot_ref[...]).astype(F32), wide), wide).astype(BF16)

        def codes(acc, acc_t):
            push(one_hot(iota((wide, wide), 1) // parts == iota((wide, wide), 0)), 0)
            pltpu.matmul_acc_lhs(acc, code[:2 * scen], load_staged_rhs=0)
            push(code, 1, transpose=True)
            pltpu.matmul_acc_lhs(
                acc_t, one_hot(iota((width, wide), 0) // parts == iota((width, wide), 1)),
                load_staged_rhs=0,
            )
            return pltpu.matmul_pop(acc)[:scen, :width], pltpu.matmul_pop(acc_t)[:, :cols]

        key, key_t = pl.run_scoped(
            codes, pltpu.ACC(0)((2 * scen, wide), F32), pltpu.ACC(1)((width, wide), F32)
        )
        key = key.astype(jnp.int32) - iota((scen, width), 1) % sb
        key_t = key_t.astype(jnp.int32) - iota((width, cols), 0) % sb

        row_code = rel_of(iota((qrows, two * width), 0))
        for sp in range(pairs):
            keys[sp] = jnp.concatenate(
                [key[sp * two + s2:sp * two + s2 + 1] + far * s2 for s2 in range(two)], axis=1
            )

        return key_t, row_code

    step = wide // rows

    tiles = slots // step

    def arrived(s, slot):
        for i, (at, lo, _) in enumerate(pieces):
            if (at, lo) == (s, slot):
                load_of(i).wait()
                if i + AHEAD < len(pieces):
                    load_of(i + AHEAD).start()

    def tile_sums(s, accs, todo):
        for t in todo:
            arrived(s, t * step)
            his, los = zip(*[split(land[s, t * step + k]) for k in range(step)])
            rhs = jnp.concatenate(
                [jnp.concatenate(his, axis=0), jnp.concatenate(los, axis=0)], axis=1
            )
            push(rhs, t % 2, t // 2 % 2, transpose=True)
            pltpu.matmul_acc_lhs(accs[t], w_two, load_staged_rhs=t // 2 % 2)

    def cell_sums(sp, accs, cells, row_code):
        outs = []
        for acc in accs:
            got = pltpu.matmul_pop(acc)[:parts]
            outs += [got[:, k * rows:(k + 1) * rows] for k in range(step)]
        dose = jnp.concatenate(outs, axis=0)
        onto = one_hot(row_code == keys[sp])
        d1 = dose.astype(BF16)
        rest = dose - d1.astype(F32)
        d2, d3 = split(rest)
        push(jnp.concatenate([d1, d2], axis=1), 0)
        push(lanes_of(d3, wide), 1)
        for cell in cells:
            pltpu.matmul_acc_lhs(cell, onto, load_staged_rhs=0)

    def keep_cells(sp, cells):
        both, third = [pltpu.matmul_pop(cell) for cell in cells]
        total = both[:, :rows] + (both[:, rows:] + third[:, :rows])
        part[:, sp] = total.reshape(dests, 8, rows)

    early = pairs - 1

    def forward(*accs):
        cells, accs = accs[:2], accs[2:]
        sets = [accs[k * two * tiles:(k + 1) * two * tiles] for k in range(2)]
        for s in range(scen):
            sp, s2 = divmod(s, two)
            accs = sets[sp % 2][s2 * tiles:(s2 + 1) * tiles]
            if s2 == 0 and sp:
                tile_sums(s, accs, range(tiles // 2))
                cell_sums(sp - 1, sets[(sp - 1) % 2], cells, row_code)
                tile_sums(s, accs, range(tiles // 2, tiles))
                keep_cells(sp - 1, cells)
                if sp == 2:
                    pl.semaphore_wait(barrier, count + 1)
                    to_mirror(vox_ref, far_vox, 2).start()
                    exchange(cut_of(part, 0, 2), cut_of(recv, 0, 2), 0)
                if sp == 3:
                    exchange(cut_of(part, 2, 1), cut_of(recv, 2, 1), 0)
            else:
                tile_sums(s, accs, range(tiles))
            if s == 0:
                key_t, row_code = place_slots()
        cell_sums(early, sets[early % 2], cells, row_code)
        keep_cells(early, cells)
        return key_t

    key_t = pl.run_scoped(
        forward,
        *[pltpu.ACC(u)((qrows, wide), F32) for u in range(2)],
        *[pltpu.ACC(t % 2)((2 * parts, wide), F32) for t in range(2 * two * tiles)],
    )
    exchange(cut_of(part, early, 1), cut_of(recv, early, 1), 0)

    pushed = slots - BY_ROWS

    def keep(s, carry):
        for b in range(pushed):
            hi, lo = split(land[s, b])
            strips = pl.ds(b * (rows // STRIP), rows // STRIP)
            ihl[s, strips, 0] = hi.reshape(rows // STRIP, STRIP, cols)
            ihl[s, strips, 1] = lo.reshape(rows // STRIP, STRIP, cols)
        return carry

    lax.fori_loop(0, scen, keep, 0)

    lane = iota((width, 2 * 128), 1)
    line = iota((width, 2 * 128), 0)
    q = lane % 128
    lane_code = jnp.where(
        jnp.logical_and(lane // 128 == (line % parts) // sb, q < qrows), rel_of(q), -1000
    )
    for s in range(scen):
        pick[s] = one_hot(key_t[:, s:s + 1] + far * (s % two) == lane_code)
    line = iota((parts, rows), 0)
    for s in range(scen):
        for k in range(BY_ROWS):
            at = (pushed + k) * parts
            own = jnp.broadcast_to(lax.rem(key_t[at:at + parts, s:s + 1], sb), line.shape) == 0
            spot_rows[s * BY_ROWS + k] = jnp.where(jnp.logical_and(own, line < sb), 1.0, 0.0)
    for load in small[3:]:
        load.wait()
    labels = lab_ref[...]
    target = jnp.zeros(labels.shape, F32)
    for k in range(presc_ref.shape[0]):
        target = jnp.where(labels == k, presc_ref[k], target)
    target = jnp.concatenate([target] * two, axis=0)
    imp = jnp.concatenate([imp_ref[...]] * two, axis=0)

    to_mirror(vox_ref, far_vox, 2).wait()
    far_rows = jnp.broadcast_to(far_vox[...][:, :1] - vr * me, (scen, rows))
    row = iota((8, rows), 0)

    def both_halves(x, sp):
        return jnp.where(row < vr, x[sp * two:sp * two + 1], x[sp * two + 1:sp * two + 2])

    named = [both_halves(far_rows, sp) == row % vr for sp in range(pairs)]
    all_slabs(came.at[0])
    field = part[REACH]
    for i in range(dests):
        if i != REACH:
            field = field + recv[i]
    excess = field - target[None]
    score = imp[None] * excess * excess
    top = jnp.max(score, axis=0)
    top = jnp.maximum(top, pltpu.roll(top, vr, 0))
    expo = jnp.exp(score - top[None])
    whole = jnp.sum(expo, axis=0)
    whole = whole + pltpu.roll(whole, vr, 0)
    coef_now = expo / whole[None] * 2.0 * imp[None] * excess
    for sp in range(pairs):
        kept = jnp.where(named[sp], coef_now[sp], 0.0)
        for s2 in range(two):
            half = jnp.where(row // vr == s2, kept, 0.0)
            asked[pl.ds(sp * two + s2, 1)] = jnp.sum(half, axis=0, keepdims=True)
    coef[...] = coef_now
    exchange(lambda i: coef, lambda i: cbuf.at[i], 1)
    out_ref[pl.ds(0, vr)] = (top + jnp.log(whole))[:vr]
    cbuf[REACH] = coef_now
    all_slabs(sent.at[0])

    to_mirror(asked, far_coef, 3).wait()
    all_slabs(came.at[1], 0)
    far_now = far_coef[...]
    pad = jnp.zeros((128 - qrows, rows), BF16)

    def picked(*accs):
        for sp in range(pairs):
            near_now = cbuf[pl.ds(0, NEAR), sp].reshape(NEAR * 8, rows)
            c_hi, c_lo = split(
                jnp.concatenate([near_now, both_halves(far_now, sp)], axis=0)
            )
            c_two = jnp.concatenate([c_hi, pad, c_lo, pad], axis=0)
            push(lanes_of(c_two, wide), sp % 2, sp // 2)
            for s2 in range(two):
                pltpu.matmul_acc_lhs(
                    accs[sp * two + s2], pick[sp * two + s2],
                    **({"load_staged_rhs": sp // 2} if s2 == 0 else {}),
                )
        return [pltpu.matmul_pop(acc)[:, :rows] for acc in accs]

    lefts = pl.run_scoped(
        picked, *[pltpu.ACC(s // two % 2)((width, wide), F32) for s in range(scen)]
    )

    coef_rows = jnp.concatenate(
        [
            jnp.sum(lefts[s][b * parts:(b + 1) * parts], axis=0, keepdims=True)
            for s in range(scen) for b in range(pushed, slots)
        ], axis=0,
    )
    coef_cols = rows_of(coef_rows, rows).T

    def by_rows(v):
        s, k = divmod(v, BY_ROWS)
        prod = land[s, pushed + k] * coef_cols[:, v:v + 1]
        tall = jnp.sum(prod.reshape(rows // 8, 8, cols), axis=0)
        return spot_rows[v] * jnp.sum(tall, axis=0, keepdims=True)

    def gather(*sums):
        count_t, count_v, done, rest = scen * pushed // step, scen * BY_ROWS, 0, 0.0
        for t in range(count_t):
            while done < count_v and (done + 1) * (count_t - 8) <= (t + 1 - 8) * count_v:
                rest = rest + by_rows(done)
                done += 1
            s, b = divmod(t * step, pushed)
            unit, stage = t % 2, t // 2 % 2
            strips = pl.ds(b * (rows // STRIP), step * (rows // STRIP))
            push(
                jnp.concatenate(
                    [ihl[s, strips, h].reshape(step * rows, cols) for h in range(2)], axis=1
                ), unit, stage,
            )
            left = jnp.concatenate(
                [lefts[s][(b + k) * parts:(b + k + 1) * parts] for k in range(step)], axis=1
            )
            pltpu.matmul_acc_lhs(
                sums[unit], jnp.concatenate([left, none], axis=0).astype(BF16),
                load_staged_rhs=stage,
            )
        return (pltpu.matmul_pop(sums[0]) + pltpu.matmul_pop(sums[1]))[:parts], rest

    acc, rest = pl.run_scoped(gather, *[pltpu.ACC(u)((2 * parts, wide), F32) for u in range(2)])
    acc = acc[:, :cols] + acc[:, cols:]
    acc = acc + rest
    out_ref[pl.ds(vr, sb)] = acc[:sb] + acc[sb:]

    all_slabs(sent.at[1], 0)


def per_device(influence, spot_weights, vox_block, spot_block, labels, importance, prescription):
    scen, slots, rows, cols = influence.shape
    sb = spot_weights.shape[0] // cols
    vr = labels.shape[0] // rows
    assert 8 % vr == 0 and 2 * vr == 8 and scen % 2 == 0 and 2 * sb == 8
    slab = (scen * vr // 8, 8, rows)
    dests = NEAR + 1
    vmem = pl.BlockSpec(memory_space=pltpu.VMEM)
    both = pl.pallas_call(
        kernel,
        out_shape=pltpu.VMEM((vr + sb, rows), F32),
        in_specs=[pl.BlockSpec(memory_space=pl.ANY)] * 7,
        out_specs=vmem,
        scratch_shapes=[
            pltpu.VMEM((sb, cols), F32),
            pltpu.VMEM(vox_block.shape, jnp.int32),
            pltpu.VMEM(spot_block.shape, jnp.int32),
            pltpu.VMEM((vr, rows), jnp.int32),
            pltpu.VMEM((vr, rows), F32),
            pltpu.SMEM(prescription.shape, F32),
            pltpu.VMEM((scen, slots, rows, cols), F32),
            pltpu.VMEM((scen, slots * rows // STRIP, 2, STRIP, cols), BF16),
            pltpu.VMEM((dests,) + slab, F32),
            pltpu.VMEM((dests,) + slab, F32),
            pltpu.VMEM(slab, F32),
            pltpu.VMEM((dests,) + slab, F32),
            pltpu.VMEM((scen, slots * 2 * sb, 256), BF16),
            pltpu.VMEM((scen // 2, 1, 2 * slots * 2 * sb), jnp.int32),
            pltpu.VMEM((scen * BY_ROWS, 2 * sb, rows), F32),
            pltpu.VMEM(vox_block.shape, jnp.int32),
            pltpu.VMEM((scen, rows), F32),
            pltpu.VMEM((scen, rows), F32),
            pltpu.SemaphoreType.DMA((4,)),
            pltpu.SemaphoreType.DMA((4,)),
        ],
        compiler_params=pltpu.CompilerParams(
            collective_id=0, has_side_effects=True, vmem_limit_bytes=56 * 1024 * 1024
        ),
    )(
        influence, spot_weights.reshape(sb, cols), vox_block, spot_block,
        labels.reshape(vr, rows), importance.reshape(vr, rows), prescription,
    )
    return both[:vr].reshape(vr * rows), both[vr:].reshape(sb * cols)


def solution(mesh):
    both = P(("groups", "spots"))
    in_specs = (
        P(None, ("groups", "spots"), None, None),
        both,
        P(None, ("groups", "spots")),
        P(None, ("groups", "spots")),
        both,
        both,
        P("groups"),
    )
    return jax.shard_map(
        per_device, mesh=mesh, in_specs=in_specs, out_specs=(both, both), check_vma=False
    )
```

```python
import jax
import jax.numpy as jnp
from jax import lax
from jax.experimental import pallas as pl
from jax.experimental.pallas import tpu as pltpu
from jax.sharding import PartitionSpec as P

REACH = 4
NEAR = 2 * REACH + 1
AHEAD = 8
STRIP = 16
BY_ROWS = 2
F32 = jnp.float32
BF16 = jnp.bfloat16
MESH = pl.DeviceIdType.MESH


def split(x):
    hi = x.astype(BF16)
    lo = (x - hi.astype(F32)).astype(BF16)
    return hi, lo


def iota(shape, dim):
    return lax.broadcasted_iota(jnp.int32, shape, dim)


def kernel(*refs):
    pl.run_scoped(
        lambda *sems: plan(*refs, *sems),
        pltpu.SemaphoreType.DMA((5,)), pltpu.SemaphoreType.DMA((6,)),
        pltpu.SemaphoreType.DMA((AHEAD,)),
    )


def plan(
    inf_ref, w_in, vox_in, spot_in, lab_in, imp_in, presc_in,
    out_ref,
    w_ref, vox_ref, spot_ref, lab_ref, imp_ref, presc_ref,
    land, ihl, part, recv, coef, cbuf, pick, keys, spot_rows,
    far_vox, asked, far_coef, far_send, far_got, came, sent, small_sem, load_sem,
):
    scen, slots, rows, cols = land.shape
    vr = lab_ref.shape[0]
    sb = w_ref.shape[0]
    two = 8 // vr
    pairs = scen // two
    dests = NEAR + 1
    qrows = dests * 8
    n = lax.axis_size("spots")
    me = lax.axis_index("spots")
    mirror = lax.rem(me + n // 2, n)

    pieces = [(0, 0, slots // 4), (0, slots // 4, slots - slots // 4)]
    pieces += [(s, h * slots // 2, slots // 2) for s in range(1, scen - 1) for h in range(2)]
    pieces += [(scen - 1, 0, slots // 2), (scen - 1, slots // 2, slots // 2)]

    def load_of(i):
        s, lo, size = pieces[i]
        block = (s, pl.ds(lo, size))
        return pltpu.make_async_copy(inf_ref.at[block], land.at[block], load_sem.at[i % AHEAD])

    small = [
        pltpu.make_async_copy(src, dst, small_sem.at[i])
        for i, (src, dst) in enumerate((
            (w_in, w_ref), (vox_in, vox_ref), (spot_in, spot_ref),
            (lab_in, lab_ref), (imp_in, imp_ref), (presc_in, presc_ref),
        ))
    ]
    for load in small[:3] + [load_of(s) for s in range(AHEAD)] + small[3:]:
        load.start()

    near = [e for e in range(-REACH, REACH + 1) if e != 0]
    order = sorted(near, key=lambda e: (-abs(e), e))

    def inside(e):
        return me + e >= 0 if e < 0 else me + e < n

    barrier = pltpu.get_barrier_semaphore()
    for e in near:
        @pl.when(inside(e))
        def _():
            pl.semaphore_signal(barrier, inc=1, device_id={"spots": me + e}, device_id_type=MESH)
    pl.semaphore_signal(barrier, inc=1, device_id={"spots": mirror}, device_id_type=MESH)

    for e in near:
        @pl.when(jnp.logical_not(inside(e)))
        def _():
            recv[e + REACH] = jnp.zeros(recv.shape[1:], F32)
            cbuf[e + REACH] = jnp.zeros(cbuf.shape[1:], F32)

    small[0].wait()
    w_hi, w_lo = split(w_ref[...])
    w_rows = jnp.concatenate([w_hi.astype(F32), w_lo.astype(F32)], axis=0)
    parts = w_rows.shape[0]
    wide = 2 * cols
    none = jnp.zeros((parts, wide), F32)
    w_two = jnp.concatenate(
        [jnp.concatenate([w_rows, w_rows], axis=1), none], axis=0
    ).astype(BF16)
    width = slots * parts

    def one_hot(mask):
        return mask.astype(F32).astype(BF16)

    def push(rhs, unit, stage=0, transpose=False):
        pltpu.matmul_push_rhs(rhs, stage, unit, transpose=transpose)

    def rows_of(x, count):
        return jnp.concatenate([x, jnp.zeros((count - x.shape[0], x.shape[1]), x.dtype)], axis=0)

    def lanes_of(x, count):
        return jnp.concatenate([x, jnp.zeros((x.shape[0], count - x.shape[1]), x.dtype)], axis=1)

    far = sb * vr * dests * 2

    def rel_of(q):
        return sb * ((q // 8) * vr + q % vr) + far * ((q % 8) // vr)

    count = sum(inside(e).astype(jnp.int32) for e in near)
    counts = sorted({sum(0 <= m + e < n for e in near) for m in range(n)})

    def near_copy(src, dst, turn, e):
        return pltpu.make_async_remote_copy(
            src_ref=src(REACH + e), dst_ref=dst(REACH - e),
            send_sem=sent.at[turn], recv_sem=came.at[turn],
            device_id={"spots": me + e}, device_id_type=MESH,
        )

    def to_mirror(src, dst, turn):
        return pltpu.make_async_remote_copy(
            src_ref=src, dst_ref=dst, send_sem=sent.at[turn], recv_sem=came.at[turn],
            device_id={"spots": mirror}, device_id_type=MESH,
        )

    def exchange(src, dst, turn):
        if turn:
            to_mirror(asked, far_coef, 3).start()
        for e in order:
            @pl.when(inside(e))
            def _():
                near_copy(src, dst, turn, e).start()

    def all_slabs(sem, more=1):
        for c in counts:
            @pl.when(count == c)
            def _():
                slabs = recv.at[pl.ds(0, c + more)]
                pltpu.make_async_copy(slabs, slabs, sem).wait()

    def cut_of(ref, lo, size):
        return lambda i: ref.at[i, pl.ds(lo, size)]

    def place_slots():
        small[1].wait()
        small[2].wait()
        vox = vox_ref[...]
        slot_id = iota(vox.shape, 1)
        rel = jnp.where(
            slot_id == 0,
            vox - vr * mirror + vr * NEAR,
            vox - vr * me + vr * REACH,
        )
        code = rows_of(lanes_of((rel * sb + spot_ref[...]).astype(F32), wide), wide).astype(BF16)

        def codes(acc, acc_t):
            push(one_hot(iota((wide, wide), 1) // parts == iota((wide, wide), 0)), 0)
            pltpu.matmul_acc_lhs(acc, code[:2 * scen], load_staged_rhs=0)
            push(code, 1, transpose=True)
            pltpu.matmul_acc_lhs(
                acc_t, one_hot(iota((width, wide), 0) // parts == iota((width, wide), 1)),
                load_staged_rhs=0,
            )
            return pltpu.matmul_pop(acc)[:scen, :width], pltpu.matmul_pop(acc_t)[:, :cols]

        key, key_t = pl.run_scoped(
            codes, pltpu.ACC(0)((2 * scen, wide), F32), pltpu.ACC(1)((width, wide), F32)
        )
        key = key.astype(jnp.int32) - iota((scen, width), 1) % sb
        key_t = key_t.astype(jnp.int32) - iota((width, cols), 0) % sb

        row_code = rel_of(iota((qrows, two * width), 0))
        for sp in range(pairs):
            keys[sp] = jnp.concatenate(
                [key[sp * two + s2:sp * two + s2 + 1] + far * s2 for s2 in range(two)], axis=1
            )

        return key_t, row_code

    step = wide // rows

    tiles = slots // step

    def arrived(s, slot):
        for i, (at, lo, _) in enumerate(pieces):
            if (at, lo) == (s, slot):
                load_of(i).wait()
                if i + AHEAD < len(pieces):
                    load_of(i + AHEAD).start()

    def tile_sums(s, accs, todo):
        for t in todo:
            arrived(s, t * step)
            his, los = zip(*[split(land[s, t * step + k]) for k in range(step)])
            rhs = jnp.concatenate(
                [jnp.concatenate(his, axis=0), jnp.concatenate(los, axis=0)], axis=1
            )
            push(rhs, t % 2, t // 2 % 2, transpose=True)
            pltpu.matmul_acc_lhs(accs[t], w_two, load_staged_rhs=t // 2 % 2)

    def cell_sums(sp, accs, cells, row_code):
        outs = []
        for acc in accs:
            got = pltpu.matmul_pop(acc)[:parts]
            outs += [got[:, k * rows:(k + 1) * rows] for k in range(step)]
        dose = jnp.concatenate(outs, axis=0)
        onto = one_hot(row_code == keys[sp])
        d1 = dose.astype(BF16)
        rest = dose - d1.astype(F32)
        d2, d3 = split(rest)
        push(jnp.concatenate([d1, d2], axis=1), 0)
        push(lanes_of(d3, wide), 1)
        for cell in cells:
            pltpu.matmul_acc_lhs(cell, onto, load_staged_rhs=0)

    def keep_cells(sp, cells):
        both, third = [pltpu.matmul_pop(cell) for cell in cells]
        total = both[:, :rows] + (both[:, rows:] + third[:, :rows])
        part[:, sp] = total.reshape(dests, 8, rows)
        far_sum = total[NEAR * 8:]
        for s2 in range(two):
            half = jnp.where(iota((8, rows), 0) // vr == s2, far_sum, 0.0)
            far_send[pl.ds(sp * two + s2, 1)] = jnp.sum(half, axis=0, keepdims=True)

    early = pairs - 1

    def forward(*accs):
        cells, accs = accs[:2], accs[2:]
        sets = [accs[k * two * tiles:(k + 1) * two * tiles] for k in range(2)]
        for s in range(scen):
            sp, s2 = divmod(s, two)
            accs = sets[sp % 2][s2 * tiles:(s2 + 1) * tiles]
            if s2 == 0 and sp:
                tile_sums(s, accs, range(tiles // 2))
                cell_sums(sp - 1, sets[(sp - 1) % 2], cells, row_code)
                tile_sums(s, accs, range(tiles // 2, tiles))
                keep_cells(sp - 1, cells)
                if sp == 2:
                    pl.semaphore_wait(barrier, count + 1)
                    to_mirror(vox_ref, far_vox, 2).start()
                    exchange(cut_of(part, 0, 2), cut_of(recv, 0, 2), 0)
                if sp == 3:
                    exchange(cut_of(part, 2, 1), cut_of(recv, 2, 1), 0)
            else:
                tile_sums(s, accs, range(tiles))
            if s == 0:
                key_t, row_code = place_slots()
        cell_sums(early, sets[early % 2], cells, row_code)
        keep_cells(early, cells)
        return key_t

    key_t = pl.run_scoped(
        forward,
        *[pltpu.ACC(u)((qrows, wide), F32) for u in range(2)],
        *[pltpu.ACC(t % 2)((2 * parts, wide), F32) for t in range(2 * two * tiles)],
    )
    to_mirror(far_send, far_got, 4).start()
    exchange(cut_of(part, early, 1), cut_of(recv, early, 1), 0)

    pushed = slots - BY_ROWS

    def keep(s, carry):
        for b in range(pushed):
            hi, lo = split(land[s, b])
            strips = pl.ds(b * (rows // STRIP), rows // STRIP)
            ihl[s, strips, 0] = hi.reshape(rows // STRIP, STRIP, cols)
            ihl[s, strips, 1] = lo.reshape(rows // STRIP, STRIP, cols)
        return carry

    lax.fori_loop(0, scen, keep, 0)

    lane = iota((width, 2 * 128), 1)
    line = iota((width, 2 * 128), 0)
    q = lane % 128
    lane_code = jnp.where(
        jnp.logical_and(lane // 128 == (line % parts) // sb, q < qrows), rel_of(q), -1000
    )
    for s in range(scen):
        pick[s] = one_hot(key_t[:, s:s + 1] + far * (s % two) == lane_code)
    line = iota((parts, rows), 0)
    for s in range(scen):
        for k in range(BY_ROWS):
            at = (pushed + k) * parts
            own = jnp.broadcast_to(lax.rem(key_t[at:at + parts, s:s + 1], sb), line.shape) == 0
            spot_rows[s * BY_ROWS + k] = jnp.where(jnp.logical_and(own, line < sb), 1.0, 0.0)
    for load in small[3:]:
        load.wait()
    labels = lab_ref[...]
    target = jnp.zeros(labels.shape, F32)
    for k in range(presc_ref.shape[0]):
        target = jnp.where(labels == k, presc_ref[k], target)
    target = jnp.concatenate([target] * two, axis=0)
    imp = jnp.concatenate([imp_ref[...]] * two, axis=0)

    to_mirror(vox_ref, far_vox, 2).wait()
    far_rows = jnp.broadcast_to(far_vox[...][:, :1] - vr * me, (scen, rows))
    row = iota((8, rows), 0)

    def both_halves(x, sp):
        return jnp.where(row < vr, x[sp * two:sp * two + 1], x[sp * two + 1:sp * two + 2])

    named = [both_halves(far_rows, sp) == row % vr for sp in range(pairs)]
    to_mirror(far_send, far_got, 4).wait()
    all_slabs(came.at[0], 0)
    far_dose = far_got[...]
    field = part[REACH]
    for i in range(NEAR):
        if i != REACH:
            field = field + recv[i]
    field = field + jnp.stack(
        [jnp.where(named[sp], both_halves(far_dose, sp), 0.0) for sp in range(pairs)]
    )
    excess = field - target[None]
    score = imp[None] * excess * excess
    top = jnp.max(score, axis=0)
    top = jnp.maximum(top, pltpu.roll(top, vr, 0))
    expo = jnp.exp(score - top[None])
    whole = jnp.sum(expo, axis=0)
    whole = whole + pltpu.roll(whole, vr, 0)
    coef_now = expo / whole[None] * 2.0 * imp[None] * excess
    for sp in range(pairs):
        kept = jnp.where(named[sp], coef_now[sp], 0.0)
        for s2 in range(two):
            half = jnp.where(row // vr == s2, kept, 0.0)
            asked[pl.ds(sp * two + s2, 1)] = jnp.sum(half, axis=0, keepdims=True)
    coef[...] = coef_now
    exchange(lambda i: coef, lambda i: cbuf.at[i], 1)
    out_ref[pl.ds(0, vr)] = (top + jnp.log(whole))[:vr]
    cbuf[REACH] = coef_now
    all_slabs(sent.at[0], 0)

    to_mirror(asked, far_coef, 3).wait()
    all_slabs(came.at[1], 0)
    far_now = far_coef[...]
    pad = jnp.zeros((128 - qrows, rows), BF16)

    def picked(*accs):
        for sp in range(pairs):
            near_now = cbuf[pl.ds(0, NEAR), sp].reshape(NEAR * 8, rows)
            c_hi, c_lo = split(
                jnp.concatenate([near_now, both_halves(far_now, sp)], axis=0)
            )
            c_two = jnp.concatenate([c_hi, pad, c_lo, pad], axis=0)
            push(lanes_of(c_two, wide), sp % 2, sp // 2)
            for s2 in range(two):
                pltpu.matmul_acc_lhs(
                    accs[sp * two + s2], pick[sp * two + s2],
                    **({"load_staged_rhs": sp // 2} if s2 == 0 else {}),
                )
        return [pltpu.matmul_pop(acc)[:, :rows] for acc in accs]

    lefts = pl.run_scoped(
        picked, *[pltpu.ACC(s // two % 2)((width, wide), F32) for s in range(scen)]
    )

    coef_rows = jnp.concatenate(
        [
            jnp.sum(lefts[s][b * parts:(b + 1) * parts], axis=0, keepdims=True)
            for s in range(scen) for b in range(pushed, slots)
        ], axis=0,
    )
    coef_cols = rows_of(coef_rows, rows).T

    def by_rows(v):
        s, k = divmod(v, BY_ROWS)
        prod = land[s, pushed + k] * coef_cols[:, v:v + 1]
        tall = jnp.sum(prod.reshape(rows // 8, 8, cols), axis=0)
        return spot_rows[v] * jnp.sum(tall, axis=0, keepdims=True)

    def gather(*sums):
        count_t, count_v, done, rest = scen * pushed // step, scen * BY_ROWS, 0, 0.0
        for t in range(count_t):
            while done < count_v and (done + 1) * (count_t - 8) <= (t + 1 - 8) * count_v:
                rest = rest + by_rows(done)
                done += 1
            s, b = divmod(t * step, pushed)
            unit, stage = t % 2, t // 2 % 2
            strips = pl.ds(b * (rows // STRIP), step * (rows // STRIP))
            push(
                jnp.concatenate(
                    [ihl[s, strips, h].reshape(step * rows, cols) for h in range(2)], axis=1
                ), unit, stage,
            )
            left = jnp.concatenate(
                [lefts[s][(b + k) * parts:(b + k + 1) * parts] for k in range(step)], axis=1
            )
            pltpu.matmul_acc_lhs(
                sums[unit], jnp.concatenate([left, none], axis=0).astype(BF16),
                load_staged_rhs=stage,
            )
        return (pltpu.matmul_pop(sums[0]) + pltpu.matmul_pop(sums[1]))[:parts], rest

    acc, rest = pl.run_scoped(gather, *[pltpu.ACC(u)((2 * parts, wide), F32) for u in range(2)])
    acc = acc[:, :cols] + acc[:, cols:]
    acc = acc + rest
    out_ref[pl.ds(vr, sb)] = acc[:sb] + acc[sb:]

    all_slabs(sent.at[1], 0)


def per_device(influence, spot_weights, vox_block, spot_block, labels, importance, prescription):
    scen, slots, rows, cols = influence.shape
    sb = spot_weights.shape[0] // cols
    vr = labels.shape[0] // rows
    assert 8 % vr == 0 and 2 * vr == 8 and scen % 2 == 0 and 2 * sb == 8
    slab = (scen * vr // 8, 8, rows)
    dests = NEAR + 1
    vmem = pl.BlockSpec(memory_space=pltpu.VMEM)
    both = pl.pallas_call(
        kernel,
        out_shape=pltpu.VMEM((vr + sb, rows), F32),
        in_specs=[pl.BlockSpec(memory_space=pl.ANY)] * 7,
        out_specs=vmem,
        scratch_shapes=[
            pltpu.VMEM((sb, cols), F32),
            pltpu.VMEM(vox_block.shape, jnp.int32),
            pltpu.VMEM(spot_block.shape, jnp.int32),
            pltpu.VMEM((vr, rows), jnp.int32),
            pltpu.VMEM((vr, rows), F32),
            pltpu.SMEM(prescription.shape, F32),
            pltpu.VMEM((scen, slots, rows, cols), F32),
            pltpu.VMEM((scen, slots * rows // STRIP, 2, STRIP, cols), BF16),
            pltpu.VMEM((dests,) + slab, F32),
            pltpu.VMEM((dests,) + slab, F32),
            pltpu.VMEM(slab, F32),
            pltpu.VMEM((dests,) + slab, F32),
            pltpu.VMEM((scen, slots * 2 * sb, 256), BF16),
            pltpu.VMEM((scen // 2, 1, 2 * slots * 2 * sb), jnp.int32),
            pltpu.VMEM((scen * BY_ROWS, 2 * sb, rows), F32),
            pltpu.VMEM(vox_block.shape, jnp.int32),
            pltpu.VMEM((scen, rows), F32),
            pltpu.VMEM((scen, rows), F32),
            pltpu.VMEM((scen, rows), F32),
            pltpu.VMEM((scen, rows), F32),
            pltpu.SemaphoreType.DMA((5,)),
        ],
        compiler_params=pltpu.CompilerParams(
            collective_id=0, has_side_effects=True, vmem_limit_bytes=56 * 1024 * 1024
        ),
    )(
        influence, spot_weights.reshape(sb, cols), vox_block, spot_block,
        labels.reshape(vr, rows), importance.reshape(vr, rows), prescription,
    )
    return both[:vr].reshape(vr * rows), both[vr:].reshape(sb * cols)


def solution(mesh):
    both = P(("groups", "spots"))
    in_specs = (
        P(None, ("groups", "spots"), None, None),
        both,
        P(None, ("groups", "spots")),
        P(None, ("groups", "spots")),
        both,
        both,
        P("groups"),
    )
    return jax.shard_map(
        per_device, mesh=mesh, in_specs=in_specs, out_specs=(both, both), check_vma=False
    )
```

```python
import jax
import jax.numpy as jnp
from jax import lax
from jax.experimental import pallas as pl
from jax.experimental.pallas import tpu as pltpu
from jax.sharding import PartitionSpec as P

REACH = 4
NEAR = 2 * REACH + 1
AHEAD = 8
STRIP = 16
BY_ROWS = 2
F32 = jnp.float32
BF16 = jnp.bfloat16
MESH = pl.DeviceIdType.MESH


def split(x):
    hi = x.astype(BF16)
    lo = (x - hi.astype(F32)).astype(BF16)
    return hi, lo


def iota(shape, dim):
    return lax.broadcasted_iota(jnp.int32, shape, dim)


def kernel(*refs):
    pl.run_scoped(
        lambda *sems: plan(*refs, *sems),
        pltpu.SemaphoreType.DMA((5,)), pltpu.SemaphoreType.DMA((6,)),
        pltpu.SemaphoreType.DMA((AHEAD,)),
    )


def plan(
    inf_ref, w_in, vox_in, spot_in, lab_in, imp_in, presc_in,
    out_ref,
    w_ref, vox_ref, spot_ref, lab_ref, imp_ref, presc_ref,
    land, ihl, part, recv, coef, cbuf, pick, keys, spot_rows,
    far_vox, asked, far_coef, far_send, far_got, came, sent, small_sem, load_sem,
):
    scen, slots, rows, cols = land.shape
    vr = lab_ref.shape[0]
    sb = w_ref.shape[0]
    two = 8 // vr
    pairs = scen // two
    dests = NEAR + 1
    qrows = dests * 8
    n = lax.axis_size("spots")
    me = lax.axis_index("spots")
    mirror = lax.rem(me + n // 2, n)

    pieces = [(0, 0, slots // 4), (0, slots // 4, slots - slots // 4)]
    pieces += [(s, h * slots // 2, slots // 2) for s in range(1, scen - 1) for h in range(2)]
    pieces += [(scen - 1, 0, slots // 2), (scen - 1, slots // 2, slots // 2)]

    def load_of(i):
        s, lo, size = pieces[i]
        block = (s, pl.ds(lo, size))
        return pltpu.make_async_copy(inf_ref.at[block], land.at[block], load_sem.at[i % AHEAD])

    small = [
        pltpu.make_async_copy(src, dst, small_sem.at[i])
        for i, (src, dst) in enumerate((
            (w_in, w_ref), (vox_in, vox_ref), (spot_in, spot_ref),
            (lab_in, lab_ref), (imp_in, imp_ref), (presc_in, presc_ref),
        ))
    ]
    for load in small[:3] + [load_of(s) for s in range(AHEAD)] + small[3:]:
        load.start()

    near = [e for e in range(-REACH, REACH + 1) if e != 0]
    order = sorted(near, key=lambda e: (-abs(e), e))

    def inside(e):
        return me + e >= 0 if e < 0 else me + e < n

    barrier = pltpu.get_barrier_semaphore()
    for e in near:
        @pl.when(inside(e))
        def _():
            pl.semaphore_signal(barrier, inc=1, device_id={"spots": me + e}, device_id_type=MESH)
    pl.semaphore_signal(barrier, inc=1, device_id={"spots": mirror}, device_id_type=MESH)

    for e in near:
        @pl.when(jnp.logical_not(inside(e)))
        def _():
            recv[e + REACH] = jnp.zeros(recv.shape[1:], F32)
            cbuf[e + REACH] = jnp.zeros(cbuf.shape[1:], F32)

    small[0].wait()
    w_hi, w_lo = split(w_ref[...])
    w_rows = jnp.concatenate([w_hi.astype(F32), w_lo.astype(F32)], axis=0)
    parts = w_rows.shape[0]
    wide = 2 * cols
    none = jnp.zeros((parts, wide), F32)
    w_two = jnp.concatenate(
        [jnp.concatenate([w_rows, w_rows], axis=1), none], axis=0
    ).astype(BF16)
    width = slots * parts

    def one_hot(mask):
        return mask.astype(F32).astype(BF16)

    def push(rhs, unit, stage=0, transpose=False):
        pltpu.matmul_push_rhs(rhs, stage, unit, transpose=transpose)

    def rows_of(x, count):
        return jnp.concatenate([x, jnp.zeros((count - x.shape[0], x.shape[1]), x.dtype)], axis=0)

    def lanes_of(x, count):
        return jnp.concatenate([x, jnp.zeros((x.shape[0], count - x.shape[1]), x.dtype)], axis=1)

    far = sb * vr * dests * 2

    def rel_of(q):
        return sb * ((q // 8) * vr + q % vr) + far * ((q % 8) // vr)

    count = sum(inside(e).astype(jnp.int32) for e in near)
    counts = sorted({sum(0 <= m + e < n for e in near) for m in range(n)})

    def near_copy(src, dst, turn, e):
        return pltpu.make_async_remote_copy(
            src_ref=src(REACH + e), dst_ref=dst(REACH - e),
            send_sem=sent.at[turn], recv_sem=came.at[turn],
            device_id={"spots": me + e}, device_id_type=MESH,
        )

    def to_mirror(src, dst, turn):
        return pltpu.make_async_remote_copy(
            src_ref=src, dst_ref=dst, send_sem=sent.at[turn], recv_sem=came.at[turn],
            device_id={"spots": mirror}, device_id_type=MESH,
        )

    def exchange(src, dst, turn):
        if turn:
            to_mirror(asked, far_coef, 3).start()
        for e in order:
            @pl.when(inside(e))
            def _():
                near_copy(src, dst, turn, e).start()

    def all_slabs(sem, more=1):
        for c in counts:
            @pl.when(count == c)
            def _():
                slabs = recv.at[pl.ds(0, c + more)]
                pltpu.make_async_copy(slabs, slabs, sem).wait()

    def cut_of(ref, lo, size):
        return lambda i: ref.at[i, pl.ds(lo, size)]

    def place_slots():
        small[1].wait()
        small[2].wait()
        vox = vox_ref[...]
        slot_id = iota(vox.shape, 1)
        rel = jnp.where(
            slot_id == 0,
            vox - vr * mirror + vr * NEAR,
            vox - vr * me + vr * REACH,
        )
        code = rows_of(lanes_of((rel * sb + spot_ref[...]).astype(F32), wide), wide).astype(BF16)

        def codes(acc, acc_t):
            push(one_hot(iota((wide, wide), 1) // parts == iota((wide, wide), 0)), 0)
            pltpu.matmul_acc_lhs(acc, code[:2 * scen], load_staged_rhs=0)
            push(code, 1, transpose=True)
            pltpu.matmul_acc_lhs(
                acc_t, one_hot(iota((width, wide), 0) // parts == iota((width, wide), 1)),
                load_staged_rhs=0,
            )
            return pltpu.matmul_pop(acc)[:scen, :width], pltpu.matmul_pop(acc_t)[:, :cols]

        key, key_t = pl.run_scoped(
            codes, pltpu.ACC(0)((2 * scen, wide), F32), pltpu.ACC(1)((width, wide), F32)
        )
        key = key.astype(jnp.int32) - iota((scen, width), 1) % sb
        key_t = key_t.astype(jnp.int32) - iota((width, cols), 0) % sb

        row_code = rel_of(iota((qrows, two * width), 0))
        for sp in range(pairs):
            keys[sp] = jnp.concatenate(
                [key[sp * two + s2:sp * two + s2 + 1] + far * s2 for s2 in range(two)], axis=1
            )

        return key_t, row_code

    step = wide // rows

    tiles = slots // step

    def arrived(s, slot):
        for i, (at, lo, _) in enumerate(pieces):
            if (at, lo) == (s, slot):
                load_of(i).wait()
                if i + AHEAD < len(pieces):
                    load_of(i + AHEAD).start()

    def tile_sums(s, accs, todo):
        for t in todo:
            arrived(s, t * step)
            his, los = zip(*[split(land[s, t * step + k]) for k in range(step)])
            rhs = jnp.concatenate(
                [jnp.concatenate(his, axis=0), jnp.concatenate(los, axis=0)], axis=1
            )
            push(rhs, t % 2, t // 2 % 2, transpose=True)
            pltpu.matmul_acc_lhs(accs[t], w_two, load_staged_rhs=t // 2 % 2)

    def cell_sums(sp, accs, cells, row_code):
        outs = []
        for acc in accs:
            got = pltpu.matmul_pop(acc)[:parts]
            outs += [got[:, k * rows:(k + 1) * rows] for k in range(step)]
        dose = jnp.concatenate(outs, axis=0)
        onto = one_hot(row_code == keys[sp])
        d1 = dose.astype(BF16)
        rest = dose - d1.astype(F32)
        d2, d3 = split(rest)
        push(jnp.concatenate([d1, d2], axis=1), 0)
        push(lanes_of(d3, wide), 1)
        for cell in cells:
            pltpu.matmul_acc_lhs(cell, onto, load_staged_rhs=0)

    def keep_cells(sp, cells):
        both, third = [pltpu.matmul_pop(cell) for cell in cells]
        total = both[:, :rows] + (both[:, rows:] + third[:, :rows])
        part[:, sp] = total.reshape(dests, 8, rows)
        far_sum = total[NEAR * 8:]
        for s2 in range(two):
            half = jnp.where(iota((8, rows), 0) // vr == s2, far_sum, 0.0)
            far_send[pl.ds(sp * two + s2, 1)] = jnp.sum(half, axis=0, keepdims=True)

    early = pairs - 1

    def forward(*accs):
        cells, accs = accs[:2], accs[2:]
        sets = [accs[k * two * tiles:(k + 1) * two * tiles] for k in range(2)]
        for s in range(scen):
            sp, s2 = divmod(s, two)
            accs = sets[sp % 2][s2 * tiles:(s2 + 1) * tiles]
            if s2 == 0 and sp:
                tile_sums(s, accs, range(tiles // 2))
                cell_sums(sp - 1, sets[(sp - 1) % 2], cells, row_code)
                tile_sums(s, accs, range(tiles // 2, tiles))
                keep_cells(sp - 1, cells)
                if sp == early:
                    pl.semaphore_wait(barrier, count + 1)
                    to_mirror(vox_ref, far_vox, 2).start()
                    exchange(cut_of(part, 0, early), cut_of(recv, 0, early), 0)
            else:
                tile_sums(s, accs, range(tiles))
            if s == 0:
                key_t, row_code = place_slots()
        cell_sums(early, sets[early % 2], cells, row_code)
        keep_cells(early, cells)
        return key_t

    key_t = pl.run_scoped(
        forward,
        *[pltpu.ACC(u)((qrows, wide), F32) for u in range(2)],
        *[pltpu.ACC(t % 2)((2 * parts, wide), F32) for t in range(2 * two * tiles)],
    )
    to_mirror(far_send, far_got, 4).start()
    exchange(cut_of(part, early, 1), cut_of(recv, early, 1), 0)

    pushed = slots - BY_ROWS

    def keep(s, carry):
        for b in range(pushed):
            hi, lo = split(land[s, b])
            strips = pl.ds(b * (rows // STRIP), rows // STRIP)
            ihl[s, strips, 0] = hi.reshape(rows // STRIP, STRIP, cols)
            ihl[s, strips, 1] = lo.reshape(rows // STRIP, STRIP, cols)
        return carry

    lax.fori_loop(0, scen, keep, 0)

    lane = iota((width, 2 * 128), 1)
    line = iota((width, 2 * 128), 0)
    q = lane % 128
    lane_code = jnp.where(
        jnp.logical_and(lane // 128 == (line % parts) // sb, q < qrows), rel_of(q), -1000
    )
    for s in range(scen):
        pick[s] = one_hot(key_t[:, s:s + 1] + far * (s % two) == lane_code)
    line = iota((parts, rows), 0)
    for s in range(scen):
        for k in range(BY_ROWS):
            at = (pushed + k) * parts
            own = jnp.broadcast_to(lax.rem(key_t[at:at + parts, s:s + 1], sb), line.shape) == 0
            spot_rows[s * BY_ROWS + k] = jnp.where(jnp.logical_and(own, line < sb), 1.0, 0.0)
    for load in small[3:]:
        load.wait()
    labels = lab_ref[...]
    target = jnp.zeros(labels.shape, F32)
    for k in range(presc_ref.shape[0]):
        target = jnp.where(labels == k, presc_ref[k], target)
    target = jnp.concatenate([target] * two, axis=0)
    imp = jnp.concatenate([imp_ref[...]] * two, axis=0)

    to_mirror(vox_ref, far_vox, 2).wait()
    far_rows = jnp.broadcast_to(far_vox[...][:, :1] - vr * me, (scen, rows))
    row = iota((8, rows), 0)

    def both_halves(x, sp):
        return jnp.where(row < vr, x[sp * two:sp * two + 1], x[sp * two + 1:sp * two + 2])

    named = [both_halves(far_rows, sp) == row % vr for sp in range(pairs)]
    to_mirror(far_send, far_got, 4).wait()
    all_slabs(came.at[0], 0)
    far_dose = far_got[...]
    field = part[REACH]
    for i in range(NEAR):
        if i != REACH:
            field = field + recv[i]
    field = field + jnp.stack(
        [jnp.where(named[sp], both_halves(far_dose, sp), 0.0) for sp in range(pairs)]
    )
    excess = field - target[None]
    score = imp[None] * excess * excess
    top = jnp.max(score, axis=0)
    top = jnp.maximum(top, pltpu.roll(top, vr, 0))
    expo = jnp.exp(score - top[None])
    whole = jnp.sum(expo, axis=0)
    whole = whole + pltpu.roll(whole, vr, 0)
    coef_now = expo / whole[None] * 2.0 * imp[None] * excess
    for sp in range(pairs):
        kept = jnp.where(named[sp], coef_now[sp], 0.0)
        for s2 in range(two):
            half = jnp.where(row // vr == s2, kept, 0.0)
            asked[pl.ds(sp * two + s2, 1)] = jnp.sum(half, axis=0, keepdims=True)
    coef[...] = coef_now
    exchange(lambda i: coef, lambda i: cbuf.at[i], 1)
    out_ref[pl.ds(0, vr)] = (top + jnp.log(whole))[:vr]
    cbuf[REACH] = coef_now
    all_slabs(sent.at[0], 0)

    to_mirror(asked, far_coef, 3).wait()
    all_slabs(came.at[1], 0)
    far_now = far_coef[...]
    pad = jnp.zeros((128 - qrows, rows), BF16)

    def picked(*accs):
        for sp in range(pairs):
            near_now = cbuf[pl.ds(0, NEAR), sp].reshape(NEAR * 8, rows)
            c_hi, c_lo = split(
                jnp.concatenate([near_now, both_halves(far_now, sp)], axis=0)
            )
            c_two = jnp.concatenate([c_hi, pad, c_lo, pad], axis=0)
            push(lanes_of(c_two, wide), sp % 2, sp // 2)
            for s2 in range(two):
                pltpu.matmul_acc_lhs(
                    accs[sp * two + s2], pick[sp * two + s2],
                    **({"load_staged_rhs": sp // 2} if s2 == 0 else {}),
                )
        return [pltpu.matmul_pop(acc)[:, :rows] for acc in accs]

    lefts = pl.run_scoped(
        picked, *[pltpu.ACC(s // two % 2)((width, wide), F32) for s in range(scen)]
    )

    coef_rows = jnp.concatenate(
        [
            jnp.sum(lefts[s][b * parts:(b + 1) * parts], axis=0, keepdims=True)
            for s in range(scen) for b in range(pushed, slots)
        ], axis=0,
    )
    coef_cols = rows_of(coef_rows, rows).T

    def by_rows(v):
        s, k = divmod(v, BY_ROWS)
        prod = land[s, pushed + k] * coef_cols[:, v:v + 1]
        tall = jnp.sum(prod.reshape(rows // 8, 8, cols), axis=0)
        return spot_rows[v] * jnp.sum(tall, axis=0, keepdims=True)

    def gather(*sums):
        count_t, count_v, done, rest = scen * pushed // step, scen * BY_ROWS, 0, 0.0
        for t in range(count_t):
            while done < count_v and (done + 1) * (count_t - 8) <= (t + 1 - 8) * count_v:
                rest = rest + by_rows(done)
                done += 1
            s, b = divmod(t * step, pushed)
            unit, stage = t % 2, t // 2 % 2
            strips = pl.ds(b * (rows // STRIP), step * (rows // STRIP))
            push(
                jnp.concatenate(
                    [ihl[s, strips, h].reshape(step * rows, cols) for h in range(2)], axis=1
                ), unit, stage,
            )
            left = jnp.concatenate(
                [lefts[s][(b + k) * parts:(b + k + 1) * parts] for k in range(step)], axis=1
            )
            pltpu.matmul_acc_lhs(
                sums[unit], jnp.concatenate([left, none], axis=0).astype(BF16),
                load_staged_rhs=stage,
            )
        return (pltpu.matmul_pop(sums[0]) + pltpu.matmul_pop(sums[1]))[:parts], rest

    acc, rest = pl.run_scoped(gather, *[pltpu.ACC(u)((2 * parts, wide), F32) for u in range(2)])
    acc = acc[:, :cols] + acc[:, cols:]
    acc = acc + rest
    out_ref[pl.ds(vr, sb)] = acc[:sb] + acc[sb:]

    all_slabs(sent.at[1], 0)


def per_device(influence, spot_weights, vox_block, spot_block, labels, importance, prescription):
    scen, slots, rows, cols = influence.shape
    sb = spot_weights.shape[0] // cols
    vr = labels.shape[0] // rows
    assert 8 % vr == 0 and 2 * vr == 8 and scen % 2 == 0 and 2 * sb == 8
    slab = (scen * vr // 8, 8, rows)
    dests = NEAR + 1
    vmem = pl.BlockSpec(memory_space=pltpu.VMEM)
    both = pl.pallas_call(
        kernel,
        out_shape=pltpu.VMEM((vr + sb, rows), F32),
        in_specs=[pl.BlockSpec(memory_space=pl.ANY)] * 7,
        out_specs=vmem,
        scratch_shapes=[
            pltpu.VMEM((sb, cols), F32),
            pltpu.VMEM(vox_block.shape, jnp.int32),
            pltpu.VMEM(spot_block.shape, jnp.int32),
            pltpu.VMEM((vr, rows), jnp.int32),
            pltpu.VMEM((vr, rows), F32),
            pltpu.SMEM(prescription.shape, F32),
            pltpu.VMEM((scen, slots, rows, cols), F32),
            pltpu.VMEM((scen, slots * rows // STRIP, 2, STRIP, cols), BF16),
            pltpu.VMEM((dests,) + slab, F32),
            pltpu.VMEM((dests,) + slab, F32),
            pltpu.VMEM(slab, F32),
            pltpu.VMEM((dests,) + slab, F32),
            pltpu.VMEM((scen, slots * 2 * sb, 256), BF16),
            pltpu.VMEM((scen // 2, 1, 2 * slots * 2 * sb), jnp.int32),
            pltpu.VMEM((scen * BY_ROWS, 2 * sb, rows), F32),
            pltpu.VMEM(vox_block.shape, jnp.int32),
            pltpu.VMEM((scen, rows), F32),
            pltpu.VMEM((scen, rows), F32),
            pltpu.VMEM((scen, rows), F32),
            pltpu.VMEM((scen, rows), F32),
            pltpu.SemaphoreType.DMA((5,)),
        ],
        compiler_params=pltpu.CompilerParams(
            collective_id=0, has_side_effects=True, vmem_limit_bytes=56 * 1024 * 1024
        ),
    )(
        influence, spot_weights.reshape(sb, cols), vox_block, spot_block,
        labels.reshape(vr, rows), importance.reshape(vr, rows), prescription,
    )
    return both[:vr].reshape(vr * rows), both[vr:].reshape(sb * cols)


def solution(mesh):
    both = P(("groups", "spots"))
    in_specs = (
        P(None, ("groups", "spots"), None, None),
        both,
        P(None, ("groups", "spots")),
        P(None, ("groups", "spots")),
        both,
        both,
        P("groups"),
    )
    return jax.shard_map(
        per_device, mesh=mesh, in_specs=in_specs, out_specs=(both, both), check_vma=False
    )
```
